512 devices in a mesh: lon: 32 (over x, z_lo, core), lat: 8 (over y), lev: 2 (over z_hi).
Axes of the slice: x: 4, y: 8, z: 8 (z_hi: 2, z_lo: 4; z = z_hi * 4 + z_lo), core: 2. Of those that a mesh axis runs over, the one named last changes fastest.
Arguments:
- adjoint: float32 [4, 16, 256, 8192], P(None, 'lev', 'lat', 'lon'), may hold values from -6 to 6
- courant_lon: bfloat16 [16, 256, 8192], P('lev', 'lat', 'lon'), may hold values from -0.44921875 to 0.44921875
- courant_lat: bfloat16 [16, 256, 8192], P('lev', 'lat', 'lon'), may hold values from -0.44921875 to 0.44921875
- mixing: bfloat16 [16, 256, 8192], P('lev', 'lat', 'lon'), may hold values from 0.5 to 2000
- injection: float32 [4, 16], P(None, 'lev'), may hold values from 0.05 to 1
- prior_flux: bfloat16 [4, 256, 8192], P(None, 'lat', 'lon'), may hold values from 0.0049743652 to 0.049804688
- region_ids: int32 [256, 8192], P('lat', 'lon'), may hold values from 0 to 2047
Outputs:
- adjoint_out: float32 [4, 16, 256, 8192], P(None, 'lev', 'lat', 'lon')
- region_grad: float32 [2048, 24], P(('lon', 'lat', 'lev'))
The draws below stay inside these ranges and needn't reach their ends.
All inputs are finite; a program needn't handle non-finite values.
Results may differ from the reference program's by a relative error of at most 0.0006.
Values sent between devices are 32-bit elements; how exact they have to be, the bound alone decides.
No kernel may reach another device: no remote copies, remote signals or barrier semaphores. Data moves between devices by JAX's collectives and lax.ppermute only.
A program may use at most 64 MiB of HBM per device.

```python
import math
import jax
import jax.numpy as jnp
from jax import lax

TRACERS = 4
REGIONS = 2048
STEPS = 6
LEVELS = 16
NLAT = 256
NLON = 8192


def with_ends(array, rng, smallest, top_value):
    longest = array.shape.index(max(array.shape))
    spots = []
    for shift in (0, 1):
        where = [jax.random.randint(jax.random.fold_in(rng, axis), (), 0, length) for axis, length in enumerate(array.shape)]
        where[longest] = (where[longest] + shift) % array.shape[longest]
        spots.append(tuple(where))
    return array.at[spots[0]].set(smallest).at[spots[1]].set(top_value)


def steps_of(key, shape, cuts, least, top_value):
    def one(axis_at, shards_of):
        draws = jax.random.uniform(jax.random.fold_in(jax.random.fold_in(key, 6), axis_at), (shards_of,), jnp.float32, least / len(cuts), top_value / len(cuts))
        return jnp.repeat(jnp.exp(draws), shape[axis_at] // shards_of).reshape((-1,) + (1,) * (len(shape) - axis_at - 1))

    level = one(*cuts[0])
    for cut in cuts[1:]:
        level = level * one(*cut)
    return level


def centred(key, extent, width, reach, pieces=(), dtype=jnp.bfloat16):
    entries = jax.random.normal(key, extent, jnp.float32) * width
    if len(pieces) > 0:
        entries = steps_of(key, extent, pieces, -0.22, 0.18) * entries
    return jnp.clip(entries, min=-reach, max=reach).astype(dtype)


def setup_inputs(seed: int = 0) -> dict:
    keys = jax.random.split(jax.random.key(seed), 8)
    return {
        "adjoint": centred(keys[0], (TRACERS, LEVELS, NLAT, NLON), 1.0, 6.0, ((1, 2), (2, 8), (3, 32)), jnp.float32),
        "courant_lon": jnp.clip(jax.random.uniform(keys[1], (LEVELS, NLAT, NLON), jnp.float32, -0.44921875, 0.44921875) * steps_of(keys[1], (LEVELS, NLAT, NLON), ((0, 2), (1, 8), (2, 32)), -0.4, 0.0), -0.44921875, 0.44921875).astype(jnp.bfloat16),
        "courant_lat": jnp.clip(jax.random.uniform(keys[2], (LEVELS, NLAT, NLON), jnp.float32, -0.44921875, 0.44921875) * steps_of(keys[2], (LEVELS, NLAT, NLON), ((0, 2), (1, 8), (2, 32)), -0.4, 0.0), -0.44921875, 0.44921875).astype(jnp.bfloat16),
        "mixing": jnp.clip(jnp.exp(math.log(2000.0) - 8.2940496 * jax.random.uniform(keys[3], (LEVELS, NLAT, NLON), jnp.float32) ** steps_of(keys[3], (LEVELS, NLAT, NLON), ((0, 2), (1, 8), (2, 32)), -0.2, 0.2)), 0.5, 2000.0).astype(jnp.bfloat16),
        "injection": jnp.clip(jnp.exp(math.log(1.0) - 2.9957323 * jax.random.uniform(keys[4], (TRACERS, LEVELS), jnp.float32) ** steps_of(keys[4], (TRACERS, LEVELS), ((1, 2),), -0.2, 0.2)), 0.05, 1.0),
        "prior_flux": jnp.clip(jnp.exp(math.log(0.049804688) - 2.3038113 * jax.random.uniform(keys[5], (TRACERS, NLAT, NLON), jnp.float32) ** steps_of(keys[5], (TRACERS, NLAT, NLON), ((1, 8), (2, 32)), -0.2, 0.2)), 0.0049743652, 0.049804688).astype(jnp.bfloat16),
        "region_ids": with_ends(jax.random.randint(keys[6], (NLAT, NLON), 0, REGIONS), jax.random.fold_in(keys[6], 1), 0, REGIONS - 1).astype(jnp.int32),
    }


def pivot_step(carried, pair):
    below, above = pair
    inverse = 1.0 / (1.0 + above + below * (1.0 + carried))
    cprime = -above * inverse
    return cprime, (inverse, cprime)


def eliminate_step(carried, item):
    rhs_level, below, inverse = item
    carried = (rhs_level + below * carried) * inverse
    return carried, carried


def substitute_step(carried, item):
    reduced_level, cprime = item
    carried = reduced_level - cprime * carried
    return carried, carried


def advect(tracer_field, east_rate, west_rate, north_rate, south_rate):
    east_cells = jnp.roll(tracer_field, -1, axis=3)
    west_cells = jnp.roll(tracer_field, 1, axis=3)
    zero_row = jnp.zeros_like(tracer_field[:, :, :1])
    north_cells = jnp.concatenate([tracer_field[:, :, 1:], zero_row], axis=2)
    south_cells = jnp.concatenate([zero_row, tracer_field[:, :, :-1]], axis=2)
    return (tracer_field + east_rate * (east_cells - tracer_field) + west_rate * (west_cells - tracer_field)
            + north_rate * (north_cells - tracer_field) + south_rate * (south_cells - tracer_field))


def reference(adjoint, courant_lon, courant_lat, mixing, injection, prior_flux, region_ids):
    mixing_f32 = mixing.astype(jnp.float32)
    kabove = jnp.concatenate([mixing_f32[:-1], jnp.zeros_like(mixing_f32[:1])], axis=0)
    kbelow = jnp.concatenate([jnp.zeros_like(mixing_f32[:1]), kabove[:-1]], axis=0)
    start_plane = jnp.zeros_like(kabove[0])
    _, (inverse, cprime) = lax.scan(pivot_step, start_plane, (kbelow, kabove))
    lon_wind = courant_lon.astype(jnp.float32)
    lat_wind = courant_lat.astype(jnp.float32)
    east_rate = jnp.maximum(lon_wind, 0.0)
    west_rate = jnp.maximum(-lon_wind, 0.0)
    north_rate = jnp.maximum(lat_wind, 0.0)
    south_rate = jnp.maximum(-lat_wind, 0.0)
    flux_weight = prior_flux.astype(jnp.float32)
    tracer_zero = jnp.zeros_like(adjoint[:, 0])
    current = adjoint
    weight_rows = []
    for step in range(STEPS):
        by_level = jnp.moveaxis(current, 1, 0)
        _, reduced = lax.scan(eliminate_step, tracer_zero, (by_level, kbelow, inverse))
        _, solved = lax.scan(substitute_step, tracer_zero, (reduced, cprime), reverse=True)
        solved = jnp.moveaxis(solved, 0, 1)
        weight_rows.append(flux_weight * jnp.einsum("tl,tlab->tab", injection, solved, precision=lax.Precision.HIGHEST))
        current = advect(solved, east_rate, west_rate, north_rate, south_rate)
    weights = jnp.concatenate(weight_rows, axis=0).reshape(STEPS * TRACERS, -1)
    region_grad = jax.ops.segment_sum(weights.T, region_ids.reshape(-1), num_segments=REGIONS)
    return current, region_grad
```

```python
import jax
import jax.numpy as jnp
from jax import lax
from jax.experimental import pallas as pl
from jax.experimental.pallas import tpu as pltpu
from jax.sharding import PartitionSpec as P

STEPS = 6
TRACERS = 4
FIELDS = TRACERS + 3
HERE = 8
LEVELS = 16
ROWS = 32
HALF = 128
EDGE = 8
TALL = ROWS + 2 * EDGE
WIDE = 2 * HALF
MAIN = FIELDS * HERE
STRIP = 2 * MAIN + 2 * FIELDS
HI = 256
LO = 8
SLOT = 32

VMEM = pl.BlockSpec(memory_space=pltpu.VMEM)
SMEM = pl.BlockSpec(memory_space=pltpu.SMEM)
PARAMS = pltpu.CompilerParams(vmem_limit_bytes=56 * 1024 * 1024)


def call(kernel, out_shape, operands, scalars, scratch=()):
    specs = [SMEM] * scalars + [VMEM] * (len(operands) - scalars)
    many = isinstance(out_shape, (tuple, list))
    return pl.pallas_call(
        kernel,
        out_shape=out_shape,
        in_specs=specs,
        out_specs=tuple(VMEM for _ in out_shape) if many else VMEM,
        scratch_shapes=list(scratch),
        compiler_params=PARAMS,
        name=kernel.__name__,
    )(*operands)


def f32(*shape):
    return jax.ShapeDtypeStruct(shape, jnp.float32)


def half_at(which):
    return pl.ds(pl.multiple_of(which * HALF, HALF), HALF)


def own_plane(refs, field, level, rows, lanes):
    adjoint, lon_wind, lat_wind, mixing = refs
    if field < TRACERS:
        return adjoint[field, level, rows, lanes]
    ref = (lon_wind, lat_wind, mixing)[field - TRACERS]
    return ref[level, rows, lanes].astype(jnp.float32)


def pack(side, injection, adjoint, lon_wind, lat_wind, mixing, to_partner, edge_mine, edge_other):
    refs = (adjoint, lon_wind, lat_wind, mixing)
    k = side[0]
    mine = half_at(k)
    other = half_at(1 - k)
    rows = slice(0, ROWS)
    slot = lax.broadcasted_iota(jnp.int32, (ROWS, HALF), 1) // (2 * EDGE)
    for field in range(FIELDS):
        packed_mine = jnp.zeros((ROWS, HALF), jnp.float32)
        packed_other = jnp.zeros((ROWS, HALF), jnp.float32)
        for level in range(HERE):
            shift = (2 * EDGE * level + EDGE) % HALF
            plane_mine = own_plane(refs, field, level, rows, mine)
            plane_other = own_plane(refs, field, level, rows, other)
            to_partner[field * HERE + level] = plane_other
            packed_mine = jnp.where(slot == level, pltpu.roll(plane_mine, shift, 1), packed_mine)
            packed_other = jnp.where(slot == level, pltpu.roll(plane_other, shift, 1), packed_other)
        to_partner[MAIN + field] = packed_mine
        edge_mine[field] = packed_mine
        edge_other[field] = packed_other
    for tracer in range(TRACERS):
        for level in range(HERE):
            row = tracer * HERE + level
            to_partner[MAIN + FIELDS, row : row + 1, :] = jnp.full((1, HALF), injection[tracer, level], jnp.float32)


def strips(side, adjoint, lon_wind, lat_wind, mixing, partner, edge_other, lon_same, lon_cross, first, last, edges):
    refs = (adjoint, lon_wind, lat_wind, mixing)
    k = side[0]
    mine = half_at(k)
    head = slice(0, EDGE)
    tail = slice(ROWS - EDGE, ROWS)
    for field in range(FIELDS):
        for level in range(HERE):
            at = field * HERE + level
            if field < TRACERS:
                first[at] = adjoint[field, level, head, mine]
                last[at] = adjoint[field, level, tail, mine]
            else:
                plane = own_plane(refs, field, level, slice(0, ROWS), mine)
                first[at] = plane[head]
                last[at] = plane[tail]
    first[MAIN : 2 * MAIN] = partner[0:MAIN, head, :]
    last[MAIN : 2 * MAIN] = partner[0:MAIN, tail, :]
    lane = lax.broadcasted_iota(jnp.int32, (ROWS, HALF), 1)
    inner = ((lane // EDGE) % 2) != k
    for field in range(FIELDS):
        for group, near, far in ((0, edge_other[field], lon_same[field]), (1, partner[MAIN + field], lon_cross[field])):
            merged = jnp.where(inner, near, far)
            at = group * FIELDS + field
            edges[at] = merged
            first[2 * MAIN + at] = merged[head]
            last[2 * MAIN + at] = merged[tail]


def steps(
    side, injection, adjoint, lon_wind, lat_wind, mixing, partner, edges, below, above, prior,
    kept, returned, weights,
    field_ref, lon_ref, lat_ref, kab_ref, inv_ref, cp_ref, red_ref, inj_ref,
):
    refs = (adjoint, lon_wind, lat_wind, mixing)
    k = side[0]
    mine = half_at(k)
    rows = slice(0, ROWS)
    low = slice(0, EDGE)
    mid = slice(EDGE, EDGE + ROWS)
    top = slice(EDGE + ROWS, TALL)
    main = slice(0, HALF)
    wing = slice(HALF, WIDE)

    for group in range(2):
        base = (k if group == 0 else 1 - k) * HERE
        for level in range(HERE):
            shift = (HALF - (2 * EDGE * level + EDGE)) % HALF
            for field in range(FIELDS):
                at = field * HERE + level
                plane_at = group * MAIN + at
                edge_at = group * FIELDS + field
                where = base + level
                if field < TRACERS:
                    target = field_ref.at[field, where]
                else:
                    target = (lon_ref, lat_ref, kab_ref)[field - TRACERS].at[where]
                target[low, main] = below[plane_at]
                target[top, main] = above[plane_at]
                if group == 0:
                    target[mid, main] = own_plane(refs, field, level, rows, mine)
                else:
                    target[mid, main] = partner[at]
                target[low, wing] = pltpu.roll(below[2 * MAIN + edge_at], shift, 1)
                target[mid, wing] = pltpu.roll(edges[edge_at], shift, 1)
                target[top, wing] = pltpu.roll(above[2 * MAIN + edge_at], shift, 1)
    for tracer in range(TRACERS):
        for level in range(HERE):
            row = tracer * HERE + level
            inj_ref[tracer, pl.ds(k * HERE + level, 1)] = jnp.full((1, 8, HALF), injection[tracer, level], jnp.float32)
            inj_ref[tracer, pl.ds((1 - k) * HERE + level, 1)] = jnp.broadcast_to(
                partner[MAIN + FIELDS, row : row + 1, :][None], (1, 8, HALF)
            )
    kab_ref[LEVELS - 1] = jnp.zeros((TALL, WIDE), jnp.float32)

    def pivots(tile, _):
        at = pl.ds(pl.multiple_of(tile * 8, 8), 8)
        carried = jnp.zeros((8, WIDE), jnp.float32)
        kbelow = jnp.zeros((8, WIDE), jnp.float32)
        for level in range(LEVELS):
            kabove = kab_ref[level, at, :]
            inverse = 1.0 / (1.0 + kabove + kbelow * (1.0 + carried))
            carried = -kabove * inverse
            inv_ref[level, at, :] = inverse
            cp_ref[level, at, :] = carried
            kbelow = kabove
        return 0

    lax.fori_loop(0, TALL // 8, pivots, 0)

    def one_step(step, _):
        def solve(tile, _):
            at = pl.ds(pl.multiple_of(tile * 8, 8), 8)
            carried = [jnp.zeros((8, WIDE), jnp.float32) for _ in range(TRACERS)]
            for level in range(LEVELS):
                inverse = inv_ref[level, at, :]
                if level:
                    kbelow = kab_ref[level - 1, at, :]
                for tracer in range(TRACERS):
                    rhs = field_ref[tracer, level, at, :]
                    if level:
                        rhs = rhs + kbelow * carried[tracer]
                    carried[tracer] = rhs * inverse
                    red_ref[tracer, level] = carried[tracer]
            for tracer in range(TRACERS):
                field_ref[tracer, LEVELS - 1, at, :] = carried[tracer]
            for level in reversed(range(LEVELS - 1)):
                cprime = cp_ref[level, at, :]
                for tracer in range(TRACERS):
                    carried[tracer] = red_ref[tracer, level] - cprime * carried[tracer]
                    field_ref[tracer, level, at, :] = carried[tracer]
            return 0

        lax.fori_loop(0, TALL // 8, solve, 0)

        def weigh(tile, _):
            at = pl.ds(pl.multiple_of(tile * 8 + EDGE, 8), 8)
            to = pl.ds(pl.multiple_of(tile * 8, 8), 8)
            for tracer in range(TRACERS):
                total = jnp.zeros((8, HALF), jnp.float32)
                for level in range(LEVELS):
                    total = total + inj_ref[tracer, level] * field_ref[tracer, level, at, main]
                weights[step * TRACERS + tracer, to, :] = total
            return 0

        lax.fori_loop(0, ROWS // 8, weigh, 0)

        def advect(level, _):
            lon = lon_ref[level]
            lat = lat_ref[level]
            east = lon > 0.0
            north = lat > 0.0
            lon = jnp.abs(lon)
            lat = jnp.abs(lat)
            centre = 1.0 - lon - lat
            for tracer in range(TRACERS):
                cells = field_ref[tracer, level]
                along = jnp.where(east, pltpu.roll(cells, WIDE - 1, 1), pltpu.roll(cells, 1, 1))
                across = jnp.where(north, pltpu.roll(cells, TALL - 1, 0), pltpu.roll(cells, 1, 0))
                field_ref[tracer, level] = centre * cells + lon * along + lat * across
            return 0

        lax.fori_loop(0, LEVELS, advect, 0)
        return 0

    lax.fori_loop(0, STEPS, one_step, 0)

    for tracer in range(TRACERS):
        flux = prior[tracer, :, mine].astype(jnp.float32)
        for step in range(STEPS):
            weights[step * TRACERS + tracer] = weights[step * TRACERS + tracer] * flux
        for level in range(HERE):
            kept[tracer, level] = field_ref[tracer, k * HERE + level, mid, main]
            returned[tracer, level] = field_ref[tracer, (1 - k) * HERE + level, mid, main]


def regions(side, weights, ids, sums, onehot, coarse, fine):
    mine = half_at(side[0])
    count = STEPS * TRACERS
    which = lax.broadcasted_iota(jnp.int32, (HI, HALF), 0)
    blank = jnp.zeros((SLOT - count, HALF), jnp.float32)
    nothing = jnp.zeros((SLOT, HALF), jnp.float32)
    for row in range(ROWS):
        at = slice(row * HALF, (row + 1) * HALF)
        region = ids[row : row + 1, mine]
        onehot[:, at] = jnp.where(which == region // LO, 1.0, 0.0).astype(jnp.bfloat16)
        value = jnp.concatenate([weights[:, row, :], blank], axis=0)
        big = value.astype(jnp.bfloat16).astype(jnp.float32)
        small = value - big
        for low in range(LO):
            here = region % LO == low
            to = slice(low * SLOT, (low + 1) * SLOT)
            coarse[to, at] = jnp.where(here, big, nothing).astype(jnp.bfloat16)
            fine[to, at] = jnp.where(here, small, nothing).astype(jnp.bfloat16)
    dims = (((1,), (1,)), ((), ()))
    total = lax.dot_general(onehot[...], coarse[...], dims, preferred_element_type=jnp.float32)
    total = total + lax.dot_general(onehot[...], fine[...], dims, preferred_element_type=jnp.float32)
    sums[0:HI] = total[:, :HALF]
    sums[HI : 2 * HI] = total[:, HALF:]


def join(side, kept, received, out):
    k = side[0]
    for tracer in range(TRACERS):
        for level in range(HERE):
            out[tracer, level, :, half_at(k)] = kept[tracer, level]
            out[tracer, level, :, half_at(1 - k)] = received[tracer, level]


def body(adjoint, courant_lon, courant_lat, mixing, injection, prior_flux, region_ids):
    lon_count = lax.axis_size("lon")
    lat_count = lax.axis_size("lat")
    side = lax.axis_index("lev").astype(jnp.int32).reshape(1)
    own = (adjoint, courant_lon, courant_lat, mixing)

    to_partner, edge_mine, edge_other = call(
        pack,
        (f32(MAIN + FIELDS + 1, ROWS, HALF), f32(FIELDS, ROWS, HALF), f32(FIELDS, ROWS, HALF)),
        (side, injection, *own),
        2,
    )
    partner = lax.ppermute(to_partner, "lev", [(0, 1), (1, 0)])
    same = []
    cross = []
    for i in range(lon_count):
        after = (i + 1) % lon_count
        same += [(2 * i, 2 * after), (2 * after + 1, 2 * i + 1)]
        cross += [(2 * i + 1, 2 * after), (2 * after, 2 * i + 1)]
    lon_same = lax.ppermute(edge_other, ("lon", "lev"), same)
    lon_cross = lax.ppermute(edge_mine, ("lon", "lev"), cross)

    first, last, edges = call(
        strips,
        (f32(STRIP, EDGE, HALF), f32(STRIP, EDGE, HALF), f32(2 * FIELDS, ROWS, HALF)),
        (side, *own, partner, edge_other, lon_same, lon_cross),
        1,
    )
    below = lax.ppermute(last, "lat", [(j, j + 1) for j in range(lat_count - 1)])
    above = lax.ppermute(first, "lat", [(j + 1, j) for j in range(lat_count - 1)])

    block = (LEVELS, TALL, WIDE)
    kept, returned, weights = call(
        steps,
        (
            f32(TRACERS, HERE, ROWS, HALF),
            f32(TRACERS, HERE, ROWS, HALF),
            f32(STEPS * TRACERS, ROWS, HALF),
        ),
        (side, injection, *own, partner, edges, below, above, prior_flux),
        2,
        [
            pltpu.VMEM((TRACERS, *block), jnp.float32),
            pltpu.VMEM(block, jnp.float32),
            pltpu.VMEM(block, jnp.float32),
            pltpu.VMEM(block, jnp.float32),
            pltpu.VMEM(block, jnp.float32),
            pltpu.VMEM(block, jnp.float32),
            pltpu.VMEM((TRACERS, LEVELS, 8, WIDE), jnp.float32),
            pltpu.VMEM((TRACERS, LEVELS, 8, HALF), jnp.float32),
        ],
    )
    received = lax.ppermute(returned, "lev", [(0, 1), (1, 0)])
    sums = call(
        regions,
        f32(2 * HI, HALF),
        (side, weights, region_ids),
        1,
        [pltpu.VMEM((HI, ROWS * HALF), jnp.bfloat16) for _ in range(3)],
    )
    pieces = lax.all_to_all(sums, ("lev", "lon", "lat"), 0, 0, tiled=True)
    region_grad = jnp.sum(pieces, axis=0).reshape(-1, SLOT)[:, : STEPS * TRACERS]
    adjoint_out = call(join, f32(*adjoint.shape), (side, kept, received), 1)
    return (adjoint_out, region_grad)


def solution(mesh):
    placed = (
        P(None, "lev", "lat", "lon"),
        P("lev", "lat", "lon"),
        P("lev", "lat", "lon"),
        P("lev", "lat", "lon"),
        P(None, "lev"),
        P(None, "lat", "lon"),
        P("lat", "lon"),
    )
    return jax.shard_map(
        body,
        mesh=mesh,
        in_specs=placed,
        out_specs=(P(None, "lev", "lat", "lon"), P(("lon", "lat", "lev"), None)),
        check_vma=False,
    )
```

```python
import jax
import jax.numpy as jnp
from jax import lax
from jax.experimental import pallas as pl
from jax.experimental.pallas import tpu as pltpu
from jax.sharding import PartitionSpec as P

STEPS = 6
TRACERS = 4
FIELDS = TRACERS + 3
HERE = 8
LEVELS = 16
ROWS = 32
HALF = 128
EDGE = 8
TALL = ROWS + 2 * EDGE
WIDE = 2 * HALF
MAIN = FIELDS * HERE
STRIP = 2 * MAIN + 2 * FIELDS
HI = 256
LO = 8
SLOT = 32

VMEM = pl.BlockSpec(memory_space=pltpu.VMEM)
SMEM = pl.BlockSpec(memory_space=pltpu.SMEM)
MIB = 1024 * 1024


def call(kernel, out_shape, operands, scalars, scratch=(), limit=8):
    specs = [SMEM] * scalars + [VMEM] * (len(operands) - scalars)
    many = isinstance(out_shape, (tuple, list))
    return pl.pallas_call(
        kernel,
        out_shape=out_shape,
        in_specs=specs,
        out_specs=tuple(VMEM for _ in out_shape) if many else VMEM,
        scratch_shapes=list(scratch),
        compiler_params=pltpu.CompilerParams(vmem_limit_bytes=limit * MIB),
        name=kernel.__name__,
    )(*operands)


def f32(*shape):
    return jax.ShapeDtypeStruct(shape, jnp.float32)


def near(*shape):
    return pltpu.VMEM(shape, jnp.float32)


def hold(x):
    return pltpu.with_memory_space_constraint(x, pltpu.VMEM)


def permute(x, axes, pairs):
    return hold(lax.ppermute(x, axes, pairs))


def half_at(which):
    return pl.ds(pl.multiple_of(which * HALF, HALF), HALF)


def own_plane(refs, field, level, rows, lanes):
    adjoint, lon_wind, lat_wind, mixing = refs
    if field < TRACERS:
        return adjoint[field, level, rows, lanes]
    ref = (lon_wind, lat_wind, mixing)[field - TRACERS]
    return ref[level, rows, lanes].astype(jnp.float32)


def pack(side, injection, adjoint, lon_wind, lat_wind, mixing, to_partner, edge_mine, edge_other):
    refs = (adjoint, lon_wind, lat_wind, mixing)
    k = side[0]
    mine = half_at(k)
    other = half_at(1 - k)
    rows = slice(0, ROWS)
    slot = lax.broadcasted_iota(jnp.int32, (ROWS, HALF), 1) // (2 * EDGE)
    for field in range(FIELDS):
        packed_mine = jnp.zeros((ROWS, HALF), jnp.float32)
        packed_other = jnp.zeros((ROWS, HALF), jnp.float32)
        for level in range(HERE):
            shift = (2 * EDGE * level + EDGE) % HALF
            plane_mine = own_plane(refs, field, level, rows, mine)
            plane_other = own_plane(refs, field, level, rows, other)
            to_partner[field * HERE + level] = plane_other
            packed_mine = jnp.where(slot == level, pltpu.roll(plane_mine, shift, 1), packed_mine)
            packed_other = jnp.where(slot == level, pltpu.roll(plane_other, shift, 1), packed_other)
        to_partner[MAIN + field] = packed_mine
        edge_mine[field] = packed_mine
        edge_other[field] = packed_other
    for tracer in range(TRACERS):
        for level in range(HERE):
            row = tracer * HERE + level
            to_partner[MAIN + FIELDS, row : row + 1, :] = jnp.full((1, HALF), injection[tracer, level], jnp.float32)


def strips(side, adjoint, lon_wind, lat_wind, mixing, partner, edge_other, lon_same, lon_cross, first, last, edges):
    refs = (adjoint, lon_wind, lat_wind, mixing)
    k = side[0]
    mine = half_at(k)
    head = slice(0, EDGE)
    tail = slice(ROWS - EDGE, ROWS)
    for field in range(FIELDS):
        for level in range(HERE):
            at = field * HERE + level
            if field < TRACERS:
                first[at] = adjoint[field, level, head, mine]
                last[at] = adjoint[field, level, tail, mine]
            else:
                plane = own_plane(refs, field, level, slice(0, ROWS), mine)
                first[at] = plane[head]
                last[at] = plane[tail]
    first[MAIN : 2 * MAIN] = partner[0:MAIN, head, :]
    last[MAIN : 2 * MAIN] = partner[0:MAIN, tail, :]
    lane = lax.broadcasted_iota(jnp.int32, (ROWS, HALF), 1)
    inner = ((lane // EDGE) % 2) != k
    for field in range(FIELDS):
        for group, near, far in ((0, edge_other[field], lon_same[field]), (1, partner[MAIN + field], lon_cross[field])):
            merged = jnp.where(inner, near, far)
            at = group * FIELDS + field
            edges[at] = merged
            first[2 * MAIN + at] = merged[head]
            last[2 * MAIN + at] = merged[tail]


def steps(
    side, injection, adjoint, lon_wind, lat_wind, mixing, partner, edges, below, above, prior,
    kept, returned, weights,
    field_ref, lon_ref, lat_ref, kab_ref, inv_ref, cp_ref, red_ref, inj_ref,
):
    refs = (adjoint, lon_wind, lat_wind, mixing)
    k = side[0]
    mine = half_at(k)
    rows = slice(0, ROWS)
    low = slice(0, EDGE)
    mid = slice(EDGE, EDGE + ROWS)
    top = slice(EDGE + ROWS, TALL)
    main = slice(0, HALF)
    wing = slice(HALF, WIDE)

    for group in range(2):
        base = (k if group == 0 else 1 - k) * HERE
        for level in range(HERE):
            shift = (HALF - (2 * EDGE * level + EDGE)) % HALF
            for field in range(FIELDS):
                at = field * HERE + level
                plane_at = group * MAIN + at
                edge_at = group * FIELDS + field
                where = base + level
                if field < TRACERS:
                    target = field_ref.at[field, where]
                else:
                    target = (lon_ref, lat_ref, kab_ref)[field - TRACERS].at[where]
                target[low, main] = below[plane_at]
                target[top, main] = above[plane_at]
                if group == 0:
                    target[mid, main] = own_plane(refs, field, level, rows, mine)
                else:
                    target[mid, main] = partner[at]
                target[low, wing] = pltpu.roll(below[2 * MAIN + edge_at], shift, 1)
                target[mid, wing] = pltpu.roll(edges[edge_at], shift, 1)
                target[top, wing] = pltpu.roll(above[2 * MAIN + edge_at], shift, 1)
    for tracer in range(TRACERS):
        for level in range(HERE):
            row = tracer * HERE + level
            inj_ref[tracer, pl.ds(k * HERE + level, 1)] = jnp.full((1, 8, HALF), injection[tracer, level], jnp.float32)
            inj_ref[tracer, pl.ds((1 - k) * HERE + level, 1)] = jnp.broadcast_to(
                partner[MAIN + FIELDS, row : row + 1, :][None], (1, 8, HALF)
            )
    kab_ref[LEVELS - 1] = jnp.zeros((TALL, WIDE), jnp.float32)

    def pivots(tile, _):
        at = pl.ds(pl.multiple_of(tile * 8, 8), 8)
        carried = jnp.zeros((8, WIDE), jnp.float32)
        kbelow = jnp.zeros((8, WIDE), jnp.float32)
        for level in range(LEVELS):
            kabove = kab_ref[level, at, :]
            inverse = 1.0 / (1.0 + kabove + kbelow * (1.0 + carried))
            carried = -kabove * inverse
            inv_ref[level, at, :] = inverse
            cp_ref[level, at, :] = carried
            kbelow = kabove
        return 0

    lax.fori_loop(0, TALL // 8, pivots, 0)

    def one_step(step, _):
        def solve(tile, _):
            at = pl.ds(pl.multiple_of(tile * 8, 8), 8)
            carried = [jnp.zeros((8, WIDE), jnp.float32) for _ in range(TRACERS)]
            for level in range(LEVELS):
                inverse = inv_ref[level, at, :]
                if level:
                    kbelow = kab_ref[level - 1, at, :]
                for tracer in range(TRACERS):
                    rhs = field_ref[tracer, level, at, :]
                    if level:
                        rhs = rhs + kbelow * carried[tracer]
                    carried[tracer] = rhs * inverse
                    red_ref[tracer, level] = carried[tracer]
            for tracer in range(TRACERS):
                field_ref[tracer, LEVELS - 1, at, :] = carried[tracer]
            for level in reversed(range(LEVELS - 1)):
                cprime = cp_ref[level, at, :]
                for tracer in range(TRACERS):
                    carried[tracer] = red_ref[tracer, level] - cprime * carried[tracer]
                    field_ref[tracer, level, at, :] = carried[tracer]
            return 0

        lax.fori_loop(0, TALL // 8, solve, 0)

        def weigh(tile, _):
            at = pl.ds(pl.multiple_of(tile * 8 + EDGE, 8), 8)
            to = pl.ds(pl.multiple_of(tile * 8, 8), 8)
            for tracer in range(TRACERS):
                total = jnp.zeros((8, HALF), jnp.float32)
                for level in range(LEVELS):
                    total = total + inj_ref[tracer, level] * field_ref[tracer, level, at, main]
                weights[step * TRACERS + tracer, to, :] = total
            return 0

        lax.fori_loop(0, ROWS // 8, weigh, 0)

        def advect(level, _):
            lon = lon_ref[level]
            lat = lat_ref[level]
            east = lon > 0.0
            north = lat > 0.0
            lon = jnp.abs(lon)
            lat = jnp.abs(lat)
            centre = 1.0 - lon - lat
            for tracer in range(TRACERS):
                cells = field_ref[tracer, level]
                along = jnp.where(east, pltpu.roll(cells, WIDE - 1, 1), pltpu.roll(cells, 1, 1))
                across = jnp.where(north, pltpu.roll(cells, TALL - 1, 0), pltpu.roll(cells, 1, 0))
                field_ref[tracer, level] = centre * cells + lon * along + lat * across
            return 0

        lax.fori_loop(0, LEVELS, advect, 0)
        return 0

    lax.fori_loop(0, STEPS, one_step, 0)

    for tracer in range(TRACERS):
        flux = prior[tracer, :, mine].astype(jnp.float32)
        for step in range(STEPS):
            weights[step * TRACERS + tracer] = weights[step * TRACERS + tracer] * flux
        for level in range(HERE):
            kept[tracer, level] = field_ref[tracer, k * HERE + level, mid, main]
            returned[tracer, level] = field_ref[tracer, (1 - k) * HERE + level, mid, main]


def regions(side, weights, ids, sums, onehot, coarse, fine):
    mine = half_at(side[0])
    count = STEPS * TRACERS
    which = lax.broadcasted_iota(jnp.int32, (HI, HALF), 0)
    blank = jnp.zeros((SLOT - count, HALF), jnp.float32)
    nothing = jnp.zeros((SLOT, HALF), jnp.float32)
    for row in range(ROWS):
        at = slice(row * HALF, (row + 1) * HALF)
        region = ids[row : row + 1, mine]
        onehot[:, at] = jnp.where(which == region // LO, 1.0, 0.0).astype(jnp.bfloat16)
        value = jnp.concatenate([weights[:, row, :], blank], axis=0)
        big = value.astype(jnp.bfloat16).astype(jnp.float32)
        small = value - big
        for low in range(LO):
            here = region % LO == low
            to = slice(low * SLOT, (low + 1) * SLOT)
            coarse[to, at] = jnp.where(here, big, nothing).astype(jnp.bfloat16)
            fine[to, at] = jnp.where(here, small, nothing).astype(jnp.bfloat16)
    dims = (((1,), (1,)), ((), ()))
    total = lax.dot_general(onehot[...], coarse[...], dims, preferred_element_type=jnp.float32)
    total = total + lax.dot_general(onehot[...], fine[...], dims, preferred_element_type=jnp.float32)
    sums[pl.ds(0, HI, stride=2)] = total[:, :HALF]
    sums[pl.ds(1, HI, stride=2)] = total[:, HALF:]


def join(side, kept, received, out):
    k = side[0]
    for tracer in range(TRACERS):
        for level in range(HERE):
            out[tracer, level, :, half_at(k)] = kept[tracer, level]
            out[tracer, level, :, half_at(1 - k)] = received[tracer, level]


def body(adjoint, courant_lon, courant_lat, mixing, injection, prior_flux, region_ids):
    lon_count = lax.axis_size("lon")
    lat_count = lax.axis_size("lat")
    side = lax.axis_index("lev").astype(jnp.int32).reshape(1)
    own = (adjoint, courant_lon, courant_lat, mixing)

    to_partner, edge_mine, edge_other = call(
        pack,
        (near(MAIN + FIELDS + 1, ROWS, HALF), near(FIELDS, ROWS, HALF), near(FIELDS, ROWS, HALF)),
        (side, injection, *own),
        2,
    )
    same = []
    cross = []
    for i in range(lon_count):
        after = (i + 1) % lon_count
        same += [(2 * i, 2 * after), (2 * after + 1, 2 * i + 1)]
        cross += [(2 * i + 1, 2 * after), (2 * after, 2 * i + 1)]
    lon_same = permute(edge_other, ("lon", "lev"), same)
    lon_cross = permute(edge_mine, ("lon", "lev"), cross)

    partner = permute(to_partner, "lev", [(0, 1), (1, 0)])

    first, last, edges = call(
        strips,
        (near(STRIP, EDGE, HALF), near(STRIP, EDGE, HALF), near(2 * FIELDS, ROWS, HALF)),
        (side, *own, partner, edge_other, lon_same, lon_cross),
        1,
    )
    below = permute(last, "lat", [(j, j + 1) for j in range(lat_count - 1)])
    above = permute(first, "lat", [(j + 1, j) for j in range(lat_count - 1)])

    block = (LEVELS, TALL, WIDE)
    kept, returned, weights = call(
        steps,
        (
            near(TRACERS, HERE, ROWS, HALF),
            near(TRACERS, HERE, ROWS, HALF),
            near(STEPS * TRACERS, ROWS, HALF),
        ),
        (side, injection, *own, partner, edges, below, above, prior_flux),
        2,
        [
            pltpu.VMEM((TRACERS, *block), jnp.float32),
            pltpu.VMEM(block, jnp.float32),
            pltpu.VMEM(block, jnp.float32),
            pltpu.VMEM(block, jnp.float32),
            pltpu.VMEM(block, jnp.float32),
            pltpu.VMEM(block, jnp.float32),
            pltpu.VMEM((TRACERS, LEVELS, 8, WIDE), jnp.float32),
            pltpu.VMEM((TRACERS, LEVELS, 8, HALF), jnp.float32),
        ],
        24,
    )
    received = permute(returned, "lev", [(0, 1), (1, 0)])
    sums = call(
        regions,
        near(2 * HI, HALF),
        (side, weights, region_ids),
        1,
        [pltpu.VMEM((HI, ROWS * HALF), jnp.bfloat16) for _ in range(3)],
        12,
    )
    pieces = lax.all_to_all(sums, ("lon", "lat", "lev"), 0, 0, tiled=True)
    region_grad = jnp.sum(pieces, axis=0).reshape(-1, SLOT)[:, : STEPS * TRACERS]
    adjoint_out = call(join, f32(*adjoint.shape), (side, kept, received), 1)
    return (adjoint_out, region_grad)


def solution(mesh):
    placed = (
        P(None, "lev", "lat", "lon"),
        P("lev", "lat", "lon"),
        P("lev", "lat", "lon"),
        P("lev", "lat", "lon"),
        P(None, "lev"),
        P(None, "lat", "lon"),
        P("lat", "lon"),
    )
    return jax.shard_map(
        body,
        mesh=mesh,
        in_specs=placed,
        out_specs=(P(None, "lev", "lat", "lon"), P(("lon", "lat", "lev"), None)),
        check_vma=False,
    )
```

```python
import jax
import jax.numpy as jnp
from jax import lax
from jax.experimental import pallas as pl
from jax.experimental.pallas import tpu as pltpu
from jax.sharding import PartitionSpec as P

STEPS = 6
TRACERS = 4
WINDS = 3
FIELDS = WINDS + TRACERS
FIRST = WINDS + 2
HERE = 8
LEVELS = 16
ROWS = 32
HALF = 128
EDGE = 8
TALL = ROWS + 2 * EDGE
WIDE = 2 * HALF
CHUNK = 16
HI = 256
LO = 8
SLOT = 32

VMEM = pl.BlockSpec(memory_space=pltpu.VMEM)
SMEM = pl.BlockSpec(memory_space=pltpu.SMEM)
MIB = 1024 * 1024


def call(kernel, out_shape, operands, scalars, scratch=(), limit=8):
    specs = [SMEM] * scalars + [VMEM] * (len(operands) - scalars)
    many = isinstance(out_shape, (tuple, list))
    return pl.pallas_call(
        kernel,
        out_shape=out_shape,
        in_specs=specs,
        out_specs=tuple(VMEM for _ in out_shape) if many else VMEM,
        scratch_shapes=list(scratch),
        compiler_params=pltpu.CompilerParams(vmem_limit_bytes=limit * MIB),
        name=kernel.__name__,
    )(*operands)


def f32(*shape):
    return jax.ShapeDtypeStruct(shape, jnp.float32)


def near(*shape):
    return pltpu.VMEM(shape, jnp.float32)


def hold(x):
    return pltpu.with_memory_space_constraint(x, pltpu.VMEM)


def permute(x, axes, pairs):
    return hold(lax.ppermute(x, axes, pairs))


def half_at(which):
    return pl.ds(pl.multiple_of(which * HALF, HALF), HALF)


def own_plane(refs, field, level, rows, lanes):
    if field >= WINDS:
        return refs[WINDS][field - WINDS, level, rows, lanes]
    return refs[field][level, rows, lanes].astype(jnp.float32)


def pack(side, injection, lon_wind, lat_wind, mixing, adjoint, first_part, second_part, edge_mine, edge_other):
    refs = (lon_wind, lat_wind, mixing, adjoint)
    k = side[0]
    mine = half_at(k)
    other = half_at(1 - k)
    rows = slice(0, ROWS)
    slot = lax.broadcasted_iota(jnp.int32, (ROWS, HALF), 1) // (2 * EDGE)
    for field in range(FIELDS):
        part, begin, count = (first_part, 0, FIRST) if field < FIRST else (second_part, FIRST, FIELDS - FIRST)
        packed_mine = jnp.zeros((ROWS, HALF), jnp.float32)
        packed_other = jnp.zeros((ROWS, HALF), jnp.float32)
        for level in range(HERE):
            shift = (2 * EDGE * level + EDGE) % HALF
            plane_mine = own_plane(refs, field, level, rows, mine)
            plane_other = own_plane(refs, field, level, rows, other)
            part[(field - begin) * HERE + level] = plane_other
            packed_mine = jnp.where(slot == level, pltpu.roll(plane_mine, shift, 1), packed_mine)
            packed_other = jnp.where(slot == level, pltpu.roll(plane_other, shift, 1), packed_other)
        part[count * HERE + field - begin] = packed_mine
        edge_mine[field] = packed_mine
        edge_other[field] = packed_other
    for tracer in range(TRACERS):
        for level in range(HERE):
            row = tracer * HERE + level
            first_part[FIRST * HERE + FIRST, row : row + 1, :] = jnp.full(
                (1, HALF), injection[tracer, level], jnp.float32
            )


def inner_lanes(side):
    lane = lax.broadcasted_iota(jnp.int32, (ROWS, HALF), 1)
    return ((lane // EDGE) % 2) != side[0]


def own_strips(side, lon_wind, lat_wind, mixing, adjoint, edge_other, lon_same, first, last, edges):
    refs = (lon_wind, lat_wind, mixing, adjoint)
    mine = half_at(side[0])
    head = slice(0, EDGE)
    tail = slice(ROWS - EDGE, ROWS)
    inner = inner_lanes(side)
    for field in range(FIELDS):
        for level in range(HERE):
            at = field * HERE + level
            if field < WINDS:
                plane = own_plane(refs, field, level, slice(0, ROWS), mine)
                first[at] = plane[head]
                last[at] = plane[tail]
            else:
                first[at] = own_plane(refs, field, level, head, mine)
                last[at] = own_plane(refs, field, level, tail, mine)
        merged = jnp.where(inner, edge_other[field], lon_same[field])
        edges[field] = merged
        first[FIELDS * HERE + field] = merged[head]
        last[FIELDS * HERE + field] = merged[tail]


def part_strips(begin):
    def strips(side, partner, lon_cross, first, last, edges):
        head = slice(0, EDGE)
        tail = slice(ROWS - EDGE, ROWS)
        count = edges.shape[0]
        planes = count * HERE
        inner = inner_lanes(side)
        first[0:planes] = partner[0:planes, head, :]
        last[0:planes] = partner[0:planes, tail, :]
        for field in range(count):
            merged = jnp.where(inner, partner[planes + field], lon_cross[begin + field])
            edges[field] = merged
            first[planes + field] = merged[head]
            last[planes + field] = merged[tail]

    return strips


CORE = slice(0, HALF)
WING = slice(HALF, WIDE)


def place(target, main, edge, shift):
    for rows, source, rim in zip(((0, EDGE), (EDGE, EDGE + ROWS), (EDGE + ROWS, TALL)), main, edge):
        at = slice(*rows)
        target[at, CORE] = source
        target[at, WING] = pltpu.roll(rim, shift, 1)


def gather(k, refs, begin, count, target_of, partner, own_edges, edges, own_below, own_above, below, above):
    mine = half_at(k)
    for group in range(2):
        base = (k if group == 0 else 1 - k) * HERE
        for level in range(HERE):
            shift = (HALF - (2 * EDGE * level + EDGE)) % HALF
            for field in range(begin, begin + count):
                if group == 0:
                    at = field * HERE + level
                    rim = FIELDS * HERE + field
                    middle = own_plane(refs, field, level, slice(0, ROWS), mine)
                    main = (own_below[at], middle, own_above[at])
                    edge = (own_below[rim], own_edges[field], own_above[rim])
                else:
                    at = (field - begin) * HERE + level
                    rim = count * HERE + field - begin
                    main = (below[at], partner[at], above[at])
                    edge = (below[rim], edges[field - begin], above[rim])
                place(target_of(field, base + level), main, edge, shift)


def integrate(k, count, prior, first_tracer, kept, returned, weights, field_ref, solved_ref, lon_ref, lat_ref, kab_ref, inv_ref, cp_ref, red_ref, inj_ref):
    def one_step(step, _):
        def solve(tile, _):
            at = pl.ds(pl.multiple_of(tile * 8, 8), 8)
            to = pl.ds(pl.multiple_of(tile * 8 + EDGE, 8), 8)
            carried = [None] * count
            for level in range(LEVELS):
                inverse = inv_ref[level, at, :]
                if level:
                    kbelow = kab_ref[level - 1, at, :]
                for tracer in range(count):
                    rhs = field_ref[tracer, level, at, :]
                    if level:
                        rhs = rhs + kbelow * carried[tracer]
                    carried[tracer] = rhs * inverse
                    red_ref[tracer, level] = carried[tracer]
            for tracer in range(count):
                solved_ref[tracer, LEVELS - 1, to, :] = carried[tracer]
            for level in reversed(range(LEVELS - 1)):
                cprime = cp_ref[level, at, :]
                for tracer in range(count):
                    carried[tracer] = red_ref[tracer, level] - cprime * carried[tracer]
                    solved_ref[tracer, level, to, :] = carried[tracer]
            return 0

        lax.fori_loop(0, TALL // 8, solve, 0)

        def weigh(tile, _):
            at = pl.ds(pl.multiple_of(tile * 8 + 2 * EDGE, 8), 8)
            to = pl.ds(pl.multiple_of(tile * 8, 8), 8)
            for tracer in range(count):
                total = jnp.zeros((8, HALF), jnp.float32)
                for level in range(LEVELS):
                    total = total + inj_ref[first_tracer + tracer, level] * solved_ref[tracer, level, at, CORE]
                weights[step * count + tracer, to, :] = total
            return 0

        lax.fori_loop(0, ROWS // 8, weigh, 0)

        lane = lax.broadcasted_iota(jnp.int32, (CHUNK, HALF), 1)
        left = lane == 0
        right = lane == HALF - 1

        def advect(level, _):
            for start in range(0, TALL, CHUNK):
                rows = slice(start, start + CHUNK)
                centre = slice(EDGE + start, EDGE + start + CHUNK)
                north_rows = slice(EDGE + start + 1, EDGE + start + CHUNK + 1)
                south_rows = slice(EDGE + start - 1, EDGE + start + CHUNK - 1)
                rates = []
                for side in (CORE, WING):
                    lon = lon_ref[level, rows, side]
                    lat = lat_ref[level, rows, side]
                    rates.append((lon > 0.0, lat > 0.0, jnp.abs(lon), jnp.abs(lat)))
                for tracer in range(count):
                    cells = [solved_ref[tracer, level, centre, side] for side in (CORE, WING)]
                    ahead = [pltpu.roll(c, HALF - 1, 1) for c in cells]
                    behind = [pltpu.roll(c, 1, 1) for c in cells]
                    for i, side in enumerate((CORE, WING)):
                        east, north, lon, lat = rates[i]
                        along = jnp.where(
                            east,
                            jnp.where(right, ahead[1 - i], ahead[i]),
                            jnp.where(left, behind[1 - i], behind[i]),
                        )
                        across = jnp.where(
                            north,
                            solved_ref[tracer, level, north_rows, side],
                            solved_ref[tracer, level, south_rows, side],
                        )
                        field_ref[tracer, level, rows, side] = (
                            cells[i] + lon * (along - cells[i]) + lat * (across - cells[i])
                        )
            return 0

        lax.fori_loop(0, LEVELS, advect, 0)
        return 0

    solved_ref[:, :, 0:EDGE, :] = jnp.zeros((count, LEVELS, EDGE, WIDE), jnp.float32)
    solved_ref[:, :, EDGE + TALL :, :] = jnp.zeros((count, LEVELS, EDGE, WIDE), jnp.float32)
    lax.fori_loop(0, STEPS, one_step, 0)

    mine = half_at(k)
    inside = slice(EDGE, EDGE + ROWS)
    for tracer in range(count):
        flux = prior[first_tracer + tracer, :, mine].astype(jnp.float32)
        for step in range(STEPS):
            weights[step * count + tracer] = weights[step * count + tracer] * flux
        for level in range(HERE):
            kept[tracer, level] = field_ref[tracer, k * HERE + level, inside, CORE]
            returned[tracer, level] = field_ref[tracer, (1 - k) * HERE + level, inside, CORE]


def first_steps(
    side, injection, lon_wind, lat_wind, mixing, adjoint, partner, own_edges, edges,
    own_below, own_above, below, above, prior,
    kept, returned, weights, lon_ref, lat_ref, kab_ref, inv_ref, cp_ref, inj_ref,
    field_ref, solved_ref, red_ref,
):
    k = side[0]
    refs = (lon_wind, lat_wind, mixing, adjoint)

    def target_of(field, level):
        if field >= WINDS:
            return field_ref.at[field - WINDS, level]
        return (lon_ref, lat_ref, kab_ref)[field].at[level]

    gather(k, refs, 0, FIRST, target_of, partner, own_edges, edges, own_below, own_above, below, above)
    for tracer in range(TRACERS):
        for level in range(HERE):
            row = tracer * HERE + level
            inj_ref[tracer, pl.ds(k * HERE + level, 1)] = jnp.full((1, 8, HALF), injection[tracer, level], jnp.float32)
            inj_ref[tracer, pl.ds((1 - k) * HERE + level, 1)] = jnp.broadcast_to(
                partner[FIRST * HERE + FIRST, row : row + 1, :][None], (1, 8, HALF)
            )
    kab_ref[LEVELS - 1] = jnp.zeros((TALL, WIDE), jnp.float32)

    def pivots(tile, _):
        at = pl.ds(pl.multiple_of(tile * 8, 8), 8)
        carried = jnp.zeros((8, WIDE), jnp.float32)
        kbelow = jnp.zeros((8, WIDE), jnp.float32)
        for level in range(LEVELS):
            kabove = kab_ref[level, at, :]
            inverse = 1.0 / (1.0 + kabove + kbelow * (1.0 + carried))
            carried = -kabove * inverse
            inv_ref[level, at, :] = inverse
            cp_ref[level, at, :] = carried
            kbelow = kabove
        return 0

    lax.fori_loop(0, TALL // 8, pivots, 0)
    integrate(
        k, FIRST - WINDS, prior, 0, kept, returned, weights,
        field_ref, solved_ref, lon_ref, lat_ref, kab_ref, inv_ref, cp_ref, red_ref, inj_ref,
    )


def second_steps(
    side, adjoint, partner, own_edges, edges, own_below, own_above, below, above, prior,
    lon_ref, lat_ref, kab_ref, inv_ref, cp_ref, inj_ref,
    kept, returned, weights, field_ref, solved_ref, red_ref,
):
    k = side[0]
    refs = (None, None, None, adjoint)
    gather(
        k, refs, FIRST, FIELDS - FIRST, lambda field, level: field_ref.at[field - FIRST, level],
        partner, own_edges, edges, own_below, own_above, below, above,
    )
    integrate(
        k, FIELDS - FIRST, prior, FIRST - WINDS, kept, returned, weights,
        field_ref, solved_ref, lon_ref, lat_ref, kab_ref, inv_ref, cp_ref, red_ref, inj_ref,
    )


def regions(side, first_weights, second_weights, ids, sums, onehot, coarse, fine, ordered):
    mine = half_at(side[0])
    count = STEPS * TRACERS
    which = lax.broadcasted_iota(jnp.int32, (HI, HALF), 0)
    blank = jnp.zeros((SLOT - count, HALF), jnp.float32)
    nothing = jnp.zeros((SLOT, HALF), jnp.float32)
    pair = TRACERS // 2
    for step in range(STEPS):
        ordered[step * TRACERS : step * TRACERS + pair] = first_weights[step * pair : (step + 1) * pair]
        ordered[step * TRACERS + pair : (step + 1) * TRACERS] = second_weights[step * pair : (step + 1) * pair]
    for row in range(ROWS):
        at = slice(row * HALF, (row + 1) * HALF)
        region = ids[row : row + 1, mine]
        onehot[:, at] = jnp.where(which == region // LO, 1.0, 0.0).astype(jnp.bfloat16)
        value = jnp.concatenate([ordered[:, row, :], blank], axis=0)
        big = value.astype(jnp.bfloat16).astype(jnp.float32)
        small = value - big
        for low in range(LO):
            here = region % LO == low
            to = slice(low * SLOT, (low + 1) * SLOT)
            coarse[to, at] = jnp.where(here, big, nothing).astype(jnp.bfloat16)
            fine[to, at] = jnp.where(here, small, nothing).astype(jnp.bfloat16)
    dims = (((1,), (1,)), ((), ()))
    total = lax.dot_general(onehot[...], coarse[...], dims, preferred_element_type=jnp.float32)
    total = total + lax.dot_general(onehot[...], fine[...], dims, preferred_element_type=jnp.float32)
    sums[pl.ds(0, HI, stride=2)] = total[:, :HALF]
    sums[pl.ds(1, HI, stride=2)] = total[:, HALF:]


def join(side, kept0, kept1, received0, received1, out):
    k = side[0]
    for tracer in range(TRACERS):
        kept, received, at = (kept0, received0, tracer) if tracer < 2 else (kept1, received1, tracer - 2)
        for level in range(HERE):
            out[tracer, level, :, half_at(k)] = kept[at, level]
            out[tracer, level, :, half_at(1 - k)] = received[at, level]


def body(adjoint, courant_lon, courant_lat, mixing, injection, prior_flux, region_ids):
    lon_count = lax.axis_size("lon")
    lat_count = lax.axis_size("lat")
    side = lax.axis_index("lev").astype(jnp.int32).reshape(1)
    own = tuple(hold(x) for x in (courant_lon, courant_lat, mixing, adjoint))
    adjoint = own[3]
    prior_flux = hold(prior_flux)

    same = []
    cross = []
    for i in range(lon_count):
        after = (i + 1) % lon_count
        same += [(2 * i, 2 * after), (2 * after + 1, 2 * i + 1)]
        cross += [(2 * i + 1, 2 * after), (2 * after, 2 * i + 1)]
    swap = [(0, 1), (1, 0)]
    north = [(j, j + 1) for j in range(lat_count - 1)]
    south = [(j + 1, j) for j in range(lat_count - 1)]

    counts = (FIRST, FIELDS - FIRST)
    parts = call(
        pack,
        (
            near(FIRST * HERE + FIRST + 1, ROWS, HALF),
            near(counts[1] * HERE + counts[1], ROWS, HALF),
            near(FIELDS, ROWS, HALF),
            near(FIELDS, ROWS, HALF),
        ),
        (side, injection, *own),
        2,
    )
    edge_mine, edge_other = parts[2:]
    lon_same = permute(edge_other, ("lon", "lev"), same)
    lon_cross = permute(edge_mine, ("lon", "lev"), cross)
    partners = [permute(part, "lev", swap) for part in parts[:2]]

    strip = FIELDS * HERE + FIELDS
    first, last, own_edges = call(
        own_strips,
        (near(strip, EDGE, HALF), near(strip, EDGE, HALF), near(FIELDS, ROWS, HALF)),
        (side, *own, edge_other, lon_same),
        1,
    )
    own_below = permute(last, "lat", north)
    own_above = permute(first, "lat", south)

    halos = []
    for group in range(2):
        count = counts[group]
        strip = count * HERE + count
        first, last, edges = call(
            part_strips(group * FIRST),
            (near(strip, EDGE, HALF), near(strip, EDGE, HALF), near(count, ROWS, HALF)),
            (side, partners[group], lon_cross),
            1,
        )
        halos.append((partners[group], own_edges, edges, own_below, own_above, permute(last, "lat", north), permute(first, "lat", south)))

    def results(group):
        tracers = TRACERS // 2
        return (near(tracers, HERE, ROWS, HALF), near(tracers, HERE, ROWS, HALF), near(STEPS * tracers, ROWS, HALF))

    block = (LEVELS, TALL, WIDE)
    scratch = [
        pltpu.VMEM((TRACERS // 2, LEVELS, TALL, WIDE), jnp.float32),
        pltpu.VMEM((TRACERS // 2, LEVELS, TALL + 2 * EDGE, WIDE), jnp.float32),
        pltpu.VMEM((TRACERS // 2, LEVELS, 8, WIDE), jnp.float32),
    ]
    outs = call(
        first_steps,
        (*results(0), *(near(*block) for _ in range(5)), near(TRACERS, LEVELS, 8, HALF)),
        (side, injection, *own, *halos[0], prior_flux),
        2,
        scratch,
        12,
    )
    kept0, returned0, weights0 = outs[:3]
    received0 = permute(returned0, "lev", swap)
    kept1, returned1, weights1 = call(
        second_steps,
        results(1),
        (side, adjoint, *halos[1], prior_flux, *outs[3:]),
        1,
        scratch,
        12,
    )
    received1 = permute(returned1, "lev", swap)
    sums = call(
        regions,
        near(2 * HI, HALF),
        (side, weights0, weights1, region_ids),
        1,
        [pltpu.VMEM((HI, ROWS * HALF), jnp.bfloat16) for _ in range(3)]
        + [pltpu.VMEM((STEPS * TRACERS, ROWS, HALF), jnp.float32)],
        12,
    )
    pieces = lax.all_to_all(sums, ("lon", "lat", "lev"), 0, 0, tiled=True)
    region_grad = jnp.sum(pieces, axis=0).reshape(-1, SLOT)[:, : STEPS * TRACERS]
    adjoint_out = call(join, f32(*adjoint.shape), (side, kept0, kept1, received0, received1), 1)
    return (adjoint_out, region_grad)


def solution(mesh):
    placed = (
        P(None, "lev", "lat", "lon"),
        P("lev", "lat", "lon"),
        P("lev", "lat", "lon"),
        P("lev", "lat", "lon"),
        P(None, "lev"),
        P(None, "lat", "lon"),
        P("lat", "lon"),
    )
    return jax.shard_map(
        body,
        mesh=mesh,
        in_specs=placed,
        out_specs=(P(None, "lev", "lat", "lon"), P(("lon", "lat", "lev"), None)),
        check_vma=False,
    )
```

```python
import jax
import jax.numpy as jnp
from jax import lax
from jax.experimental import pallas as pl
from jax.experimental.pallas import tpu as pltpu
from jax.sharding import PartitionSpec as P

STEPS = 6
TRACERS = 4
FIELDS = TRACERS + 3
HERE = 8
LEVELS = 16
ROWS = 32
HALF = 128
EDGE = 8
TALL = ROWS + 2 * EDGE
WIDE = 2 * HALF
MAIN = FIELDS * HERE
HI = 256
LO = 8
SLOT = 32

VMEM = pl.BlockSpec(memory_space=pltpu.VMEM)
SMEM = pl.BlockSpec(memory_space=pltpu.SMEM)
MIB = 1024 * 1024


def call(kernel, out_shape, operands, scalars, scratch=(), limit=8):
    specs = [SMEM] * scalars + [VMEM] * (len(operands) - scalars)
    many = isinstance(out_shape, (tuple, list))
    return pl.pallas_call(
        kernel,
        out_shape=out_shape,
        in_specs=specs,
        out_specs=tuple(VMEM for _ in out_shape) if many else VMEM,
        scratch_shapes=list(scratch),
        compiler_params=pltpu.CompilerParams(vmem_limit_bytes=limit * MIB),
        name=kernel.__name__,
    )(*operands)


def f32(*shape):
    return jax.ShapeDtypeStruct(shape, jnp.float32)


def near(*shape):
    return pltpu.VMEM(shape, jnp.float32)


def hold(x):
    return pltpu.with_memory_space_constraint(x, pltpu.VMEM)


def permute(x, axes, pairs):
    return hold(lax.ppermute(x, axes, pairs))


def half_at(which):
    return pl.ds(pl.multiple_of(which * HALF, HALF), HALF)


def own_plane(refs, field, level, rows, lanes):
    adjoint, lon_wind, lat_wind, mixing = refs
    if field < TRACERS:
        return adjoint[field, level, rows, lanes]
    ref = (lon_wind, lat_wind, mixing)[field - TRACERS]
    return ref[level, rows, lanes].astype(jnp.float32)


def pack_edges(side, adjoint, lon_wind, lat_wind, mixing, edge_mine, edge_other):
    refs = (adjoint, lon_wind, lat_wind, mixing)
    k = side[0]
    mine = half_at(k)
    other = half_at(1 - k)
    rows = slice(0, ROWS)
    slot = lax.broadcasted_iota(jnp.int32, (ROWS, HALF), 1) // (2 * EDGE)
    for field in range(FIELDS):
        packed_mine = jnp.zeros((ROWS, HALF), jnp.float32)
        packed_other = jnp.zeros((ROWS, HALF), jnp.float32)
        for level in range(HERE):
            shift = (2 * EDGE * level + EDGE) % HALF
            plane_mine = own_plane(refs, field, level, rows, mine)
            plane_other = own_plane(refs, field, level, rows, other)
            packed_mine = jnp.where(slot == level, pltpu.roll(plane_mine, shift, 1), packed_mine)
            packed_other = jnp.where(slot == level, pltpu.roll(plane_other, shift, 1), packed_other)
        edge_mine[field] = packed_mine
        edge_other[field] = packed_other


def pack_main(side, injection, adjoint, lon_wind, lat_wind, mixing, edge_mine, edge_other, to_partner, first, last):
    refs = (adjoint, lon_wind, lat_wind, mixing)
    k = side[0]
    mine = half_at(k)
    other = half_at(1 - k)
    rows = slice(0, ROWS)
    head = slice(0, EDGE)
    tail = slice(ROWS - EDGE, ROWS)
    for field in range(FIELDS):
        for level in range(HERE):
            at = field * HERE + level
            to_partner[at] = own_plane(refs, field, level, rows, other)
            plane = own_plane(refs, field, level, rows, mine)
            first[at] = plane[head]
            last[at] = plane[tail]
        to_partner[MAIN + field] = edge_mine[field]
        first[MAIN + field] = edge_other[field, head]
        last[MAIN + field] = edge_other[field, tail]
    for tracer in range(TRACERS):
        for level in range(HERE):
            row = tracer * HERE + level
            to_partner[MAIN + FIELDS, row : row + 1, :] = jnp.broadcast_to(
                injection[tracer : tracer + 1, level : level + 1], (1, HALF)
            )


def inner_lanes(side, rows):
    lane = lax.broadcasted_iota(jnp.int32, (rows, HALF), 1)
    return ((lane // EDGE) % 2) != side[0]


def strips(side, partner, lon_same, lon_cross, own_below, own_above, first, last, edges):
    head = slice(0, EDGE)
    tail = slice(ROWS - EDGE, ROWS)
    inner = inner_lanes(side, ROWS)
    first[0:MAIN] = partner[0:MAIN, head, :]
    last[0:MAIN] = partner[0:MAIN, tail, :]
    for field in range(FIELDS):
        merged = jnp.where(inner, partner[MAIN + field], lon_cross[field])
        edges[field] = merged
        first[MAIN + field] = merged[head]
        last[MAIN + field] = merged[tail]
        first[MAIN + FIELDS + field] = lon_same[field, head]
        last[MAIN + FIELDS + field] = lon_same[field, tail]


def steps(
    side, injection, adjoint, lon_wind, lat_wind, mixing, partner, edge_other, lon_same, edges,
    own_below, own_above, below, above, prior,
    kept, returned, weights,
    field_ref, lon_ref, lat_ref, kab_ref, inv_ref, cp_ref, red_ref, inj_ref,
):
    refs = (adjoint, lon_wind, lat_wind, mixing)
    k = side[0]
    mine = half_at(k)
    rows = slice(0, ROWS)
    low = slice(0, EDGE)
    mid = slice(EDGE, EDGE + ROWS)
    top = slice(EDGE + ROWS, TALL)
    main = slice(0, HALF)
    wing = slice(HALF, WIDE)

    inner = inner_lanes(side, ROWS)
    inner_rim = inner_lanes(side, EDGE)
    for group in range(2):
        base = (k if group == 0 else 1 - k) * HERE
        under, over = (own_below, own_above) if group == 0 else (below, above)
        for field in range(FIELDS):
            rim = MAIN + field
            if group == 0:
                far = MAIN + FIELDS + field
                edge = (
                    jnp.where(inner_rim, own_below[rim], below[far]),
                    jnp.where(inner, edge_other[field], lon_same[field]),
                    jnp.where(inner_rim, own_above[rim], above[far]),
                )
            else:
                edge = (below[rim], edges[field], above[rim])
            for level in range(HERE):
                shift = (HALF - (2 * EDGE * level + EDGE)) % HALF
                at = field * HERE + level
                where = base + level
                if field < TRACERS:
                    target = field_ref.at[field, where]
                else:
                    target = (lon_ref, lat_ref, kab_ref)[field - TRACERS].at[where]
                target[low, main] = under[at]
                target[top, main] = over[at]
                if group == 0:
                    target[mid, main] = own_plane(refs, field, level, rows, mine)
                else:
                    target[mid, main] = partner[at]
                target[low, wing] = pltpu.roll(edge[0], shift, 1)
                target[mid, wing] = pltpu.roll(edge[1], shift, 1)
                target[top, wing] = pltpu.roll(edge[2], shift, 1)
    for tracer in range(TRACERS):
        for level in range(HERE):
            row = tracer * HERE + level
            inj_ref[tracer, pl.ds(k * HERE + level, 1)] = jnp.broadcast_to(
                injection[tracer : tracer + 1, level : level + 1][None], (1, 8, HALF)
            )
            inj_ref[tracer, pl.ds((1 - k) * HERE + level, 1)] = jnp.broadcast_to(
                partner[MAIN + FIELDS, row : row + 1, :][None], (1, 8, HALF)
            )
    kab_ref[LEVELS - 1] = jnp.zeros((TALL, WIDE), jnp.float32)

    def pivots(tile, _):
        at = pl.ds(pl.multiple_of(tile * 8, 8), 8)
        carried = jnp.zeros((8, WIDE), jnp.float32)
        kbelow = jnp.zeros((8, WIDE), jnp.float32)
        for level in range(LEVELS):
            kabove = kab_ref[level, at, :]
            inverse = 1.0 / (1.0 + kabove + kbelow * (1.0 + carried))
            carried = -kabove * inverse
            inv_ref[level, at, :] = inverse
            cp_ref[level, at, :] = carried
            kbelow = kabove
        return 0

    lax.fori_loop(0, TALL // 8, pivots, 0)

    def one_step(step, _):
        def solve(tile, _):
            at = pl.ds(pl.multiple_of(tile * 8, 8), 8)
            carried = [jnp.zeros((8, WIDE), jnp.float32) for _ in range(TRACERS)]
            for level in range(LEVELS):
                inverse = inv_ref[level, at, :]
                if level:
                    kbelow = kab_ref[level - 1, at, :]
                for tracer in range(TRACERS):
                    rhs = field_ref[tracer, level, at, :]
                    if level:
                        rhs = rhs + kbelow * carried[tracer]
                    carried[tracer] = rhs * inverse
                    red_ref[tracer, level] = carried[tracer]
            for tracer in range(TRACERS):
                field_ref[tracer, LEVELS - 1, at, :] = carried[tracer]
            for level in reversed(range(LEVELS - 1)):
                cprime = cp_ref[level, at, :]
                for tracer in range(TRACERS):
                    carried[tracer] = red_ref[tracer, level] - cprime * carried[tracer]
                    field_ref[tracer, level, at, :] = carried[tracer]
            return 0

        lax.fori_loop(0, TALL // 8, solve, 0)

        def weigh(tile, _):
            at = pl.ds(pl.multiple_of(tile * 8 + EDGE, 8), 8)
            to = pl.ds(pl.multiple_of(tile * 8, 8), 8)
            for tracer in range(TRACERS):
                total = jnp.zeros((8, HALF), jnp.float32)
                for level in range(LEVELS):
                    total = total + inj_ref[tracer, level] * field_ref[tracer, level, at, main]
                weights[step * TRACERS + tracer, to, :] = total
            return 0

        lax.fori_loop(0, ROWS // 8, weigh, 0)

        def advect(level, _):
            lon = lon_ref[level]
            lat = lat_ref[level]
            east = lon > 0.0
            north = lat > 0.0
            lon = jnp.abs(lon)
            lat = jnp.abs(lat)
            centre = 1.0 - lon - lat
            for tracer in range(TRACERS):
                cells = field_ref[tracer, level]
                along = jnp.where(east, pltpu.roll(cells, WIDE - 1, 1), pltpu.roll(cells, 1, 1))
                across = jnp.where(north, pltpu.roll(cells, TALL - 1, 0), pltpu.roll(cells, 1, 0))
                field_ref[tracer, level] = centre * cells + lon * along + lat * across
            return 0

        lax.fori_loop(0, LEVELS, advect, 0)
        return 0

    lax.fori_loop(0, STEPS, one_step, 0)

    for tracer in range(TRACERS):
        flux = prior[tracer, :, mine].astype(jnp.float32)
        for step in range(STEPS):
            weights[step * TRACERS + tracer] = weights[step * TRACERS + tracer] * flux
        for level in range(HERE):
            kept[tracer, level] = field_ref[tracer, k * HERE + level, mid, main]
            returned[tracer, level] = field_ref[tracer, (1 - k) * HERE + level, mid, main]


def regions(side, weights, ids, sums, onehot, coarse, fine):
    mine = half_at(side[0])
    count = STEPS * TRACERS
    which = lax.broadcasted_iota(jnp.int32, (HI, HALF), 0)
    blank = jnp.zeros((SLOT - count, HALF), jnp.float32)
    nothing = jnp.zeros((SLOT, HALF), jnp.float32)
    for row in range(ROWS):
        at = slice(row * HALF, (row + 1) * HALF)
        region = ids[row : row + 1, mine]
        onehot[:, at] = jnp.where(which == region // LO, 1.0, 0.0).astype(jnp.bfloat16)
        value = jnp.concatenate([weights[:, row, :], blank], axis=0)
        big = value.astype(jnp.bfloat16).astype(jnp.float32)
        small = value - big
        for low in range(LO):
            here = region % LO == low
            to = slice(low * SLOT, (low + 1) * SLOT)
            coarse[to, at] = jnp.where(here, big, nothing).astype(jnp.bfloat16)
            fine[to, at] = jnp.where(here, small, nothing).astype(jnp.bfloat16)
    dims = (((1,), (1,)), ((), ()))
    total = lax.dot_general(onehot[...], coarse[...], dims, preferred_element_type=jnp.float32)
    total = total + lax.dot_general(onehot[...], fine[...], dims, preferred_element_type=jnp.float32)
    sums[pl.ds(0, HI, stride=2)] = total[:, :HALF]
    sums[pl.ds(1, HI, stride=2)] = total[:, HALF:]


def join(side, kept, received, out):
    k = side[0]
    for tracer in range(TRACERS):
        for level in range(HERE):
            out[tracer, level, :, half_at(k)] = kept[tracer, level]
            out[tracer, level, :, half_at(1 - k)] = received[tracer, level]


def body(adjoint, courant_lon, courant_lat, mixing, injection, prior_flux, region_ids):
    lon_count = lax.axis_size("lon")
    lat_count = lax.axis_size("lat")
    side = lax.axis_index("lev").astype(jnp.int32).reshape(1)
    raw = tuple(
        pltpu.with_memory_space_constraint(x, pltpu.HBM) for x in (adjoint, courant_lon, courant_lat, mixing)
    )
    own = tuple(hold(x) for x in (adjoint, courant_lon, courant_lat, mixing))
    injection = hold(injection)

    edge_mine, edge_other = call(
        pack_edges, (near(FIELDS, ROWS, HALF), near(FIELDS, ROWS, HALF)), (side, *raw), 1
    )
    same = []
    cross = []
    for i in range(lon_count):
        after = (i + 1) % lon_count
        same += [(2 * i, 2 * after), (2 * after + 1, 2 * i + 1)]
        cross += [(2 * i + 1, 2 * after), (2 * after, 2 * i + 1)]
    north = [(j, j + 1) for j in range(lat_count - 1)]
    south = [(j + 1, j) for j in range(lat_count - 1)]
    lon_cross = permute(edge_mine, ("lon", "lev"), cross)
    lon_same = permute(edge_other, ("lon", "lev"), same)

    strip = MAIN + FIELDS
    to_partner, first, last = call(
        pack_main,
        (near(MAIN + FIELDS + 1, ROWS, HALF), near(strip, EDGE, HALF), near(strip, EDGE, HALF)),
        (side, injection, *own, edge_mine, edge_other),
        1,
    )
    partner = permute(to_partner, "lev", [(0, 1), (1, 0)])
    own_below = permute(last, "lat", north)
    own_above = permute(first, "lat", south)

    strip = MAIN + 2 * FIELDS
    first, last, edges = call(
        strips,
        (near(strip, EDGE, HALF), near(strip, EDGE, HALF), near(FIELDS, ROWS, HALF)),
        (side, partner, lon_same, lon_cross, own_below, own_above),
        1,
    )
    below = permute(last, "lat", north)
    above = permute(first, "lat", south)

    block = (LEVELS, TALL, WIDE)
    kept, returned, weights = call(
        steps,
        (
            near(TRACERS, HERE, ROWS, HALF),
            near(TRACERS, HERE, ROWS, HALF),
            near(STEPS * TRACERS, ROWS, HALF),
        ),
        (
            side, injection, *own, partner, edge_other, lon_same, edges,
            own_below, own_above, below, above, hold(prior_flux),
        ),
        1,
        [
            pltpu.VMEM((TRACERS, *block), jnp.float32),
            pltpu.VMEM(block, jnp.float32),
            pltpu.VMEM(block, jnp.float32),
            pltpu.VMEM(block, jnp.float32),
            pltpu.VMEM(block, jnp.float32),
            pltpu.VMEM(block, jnp.float32),
            pltpu.VMEM((TRACERS, LEVELS, 8, WIDE), jnp.float32),
            pltpu.VMEM((TRACERS, LEVELS, 8, HALF), jnp.float32),
        ],
        24,
    )
    received = permute(returned, "lev", [(0, 1), (1, 0)])
    sums = call(
        regions,
        near(2 * HI, HALF),
        (side, weights, region_ids),
        1,
        [pltpu.VMEM((HI, ROWS * HALF), jnp.bfloat16) for _ in range(3)],
        12,
    )
    pieces = lax.all_to_all(sums, ("lon", "lat", "lev"), 0, 0, tiled=True)
    region_grad = jnp.sum(pieces, axis=0).reshape(-1, SLOT)[:, : STEPS * TRACERS]
    adjoint_out = call(join, f32(*adjoint.shape), (side, kept, received), 1)
    return (adjoint_out, region_grad)


def solution(mesh):
    placed = (
        P(None, "lev", "lat", "lon"),
        P("lev", "lat", "lon"),
        P("lev", "lat", "lon"),
        P("lev", "lat", "lon"),
        P(None, "lev"),
        P(None, "lat", "lon"),
        P("lat", "lon"),
    )
    return jax.shard_map(
        body,
        mesh=mesh,
        in_specs=placed,
        out_specs=(P(None, "lev", "lat", "lon"), P(("lon", "lat", "lev"), None)),
        check_vma=False,
    )
```

```python
import jax
import jax.numpy as jnp
from jax import lax
from jax.experimental import pallas as pl
from jax.experimental.pallas import tpu as pltpu
from jax.sharding import PartitionSpec as P

STEPS = 6
TRACERS = 4
FIELDS = TRACERS + 3
HERE = 8
LEVELS = 16
ROWS = 32
HALF = 128
EDGE = 8
TALL = ROWS + 2 * EDGE
WIDE = 2 * HALF
MAIN = FIELDS * HERE
FOLD = 2 * EDGE
PLANES = MAIN + (FIELDS + 1) // 2 + 1
HI = 256
LO = 8
SLOT = 32

VMEM = pl.BlockSpec(memory_space=pltpu.VMEM)
SMEM = pl.BlockSpec(memory_space=pltpu.SMEM)
MIB = 1024 * 1024


def call(kernel, out_shape, operands, scalars, scratch=(), limit=8, work=0):
    specs = [SMEM] * scalars + [VMEM] * (len(operands) - scalars)
    many = isinstance(out_shape, (tuple, list))
    return pl.pallas_call(
        kernel,
        out_shape=out_shape,
        in_specs=specs,
        out_specs=tuple(VMEM for _ in out_shape) if many else VMEM,
        scratch_shapes=list(scratch),
        compiler_params=pltpu.CompilerParams(vmem_limit_bytes=limit * MIB),
        name=kernel.__name__,
        cost_estimate=pl.CostEstimate(flops=work, bytes_accessed=work, transcendentals=0) if work else None,
    )(*operands)


def f32(*shape):
    return jax.ShapeDtypeStruct(shape, jnp.float32)


def near(*shape):
    return pltpu.VMEM(shape, jnp.float32)


def hold(x):
    return pltpu.with_memory_space_constraint(x, pltpu.VMEM)


def permute(x, axes, pairs):
    return hold(lax.ppermute(x, axes, pairs))


def half_at(which):
    return pl.ds(pl.multiple_of(which * HALF, HALF), HALF)


def own_plane(refs, field, level, rows, lanes):
    adjoint, lon_wind, lat_wind, mixing = refs
    if field < TRACERS:
        return adjoint[field, level, rows, lanes]
    ref = (lon_wind, lat_wind, mixing)[field - TRACERS]
    return ref[level, rows, lanes].astype(jnp.float32)


def pack_edges(side, adjoint, lon_wind, lat_wind, mixing, inner, cross, same, near):
    refs = (adjoint, lon_wind, lat_wind, mixing)
    k = side[0]
    mine = half_at(k)
    other = half_at(1 - k)
    slot = lax.broadcasted_iota(jnp.int32, (FOLD, HALF), 1) // EDGE
    upper = slice(0, FOLD)
    lower = slice(FOLD, ROWS)
    west = k == 0

    def packed(planes, begin):
        out = jnp.zeros((FOLD, HALF), jnp.float32)
        for level, plane in enumerate(planes):
            for rows, to in ((upper, level), (lower, HERE + level)):
                shift = (EDGE * to - begin) % HALF
                moved = pltpu.roll(plane[rows], shift, 1) if shift else plane[rows]
                out = jnp.where(slot == to, moved, out)
        return out

    for field in range(FIELDS):
        planes = [own_plane(refs, field, level, slice(0, ROWS), mine) for level in range(HERE)]
        low = packed(planes, 0)
        high = packed(planes, HALF - EDGE)
        inner[field] = jnp.where(west, high, low)
        cross[field] = jnp.where(west, low, high)
        planes = [own_plane(refs, field, level, slice(0, ROWS), other) for level in range(HERE)]
        low = packed(planes, 0)
        high = packed(planes, HALF - EDGE)
        same[field] = jnp.where(west, high, low)
        near[field] = jnp.where(west, low, high)


def pack_main(side, injection, adjoint, lon_wind, lat_wind, mixing, inner, to_partner):
    refs = (adjoint, lon_wind, lat_wind, mixing)
    other = half_at(1 - side[0])
    for field in range(FIELDS):
        for level in range(HERE):
            to_partner[field * HERE + level] = own_plane(refs, field, level, slice(0, ROWS), other)
        to_partner[MAIN + field // 2, pl.ds(field % 2 * FOLD, FOLD), :] = inner[field]
    for tracer in range(TRACERS):
        for level in range(HERE):
            row = tracer * HERE + level
            to_partner[PLANES - 1, row : row + 1, :] = jnp.broadcast_to(
                injection[tracer : tracer + 1, level : level + 1], (1, HALF)
            )


def own_strips(side, adjoint, lon_wind, lat_wind, mixing, near, lon_same, lon_cross, first, last):
    refs = (adjoint, lon_wind, lat_wind, mixing)
    mine = half_at(side[0])
    for field in range(FIELDS):
        for level in range(HERE):
            plane = own_plane(refs, field, level, slice(0, ROWS), mine)
            first[field * HERE + level] = plane[:EDGE]
            last[field * HERE + level] = plane[ROWS - EDGE :]
    for group, rims in enumerate((near, lon_same, lon_cross)):
        at = slice(MAIN + group * FIELDS, MAIN + (group + 1) * FIELDS)
        first[at] = rims[:, :EDGE, :]
        last[at] = rims[:, EDGE:, :]


def strips(partner, own_below, own_above, first, last):
    first[0:MAIN] = partner[0:MAIN, 0:EDGE, :]
    last[0:MAIN] = partner[0:MAIN, ROWS - EDGE : ROWS, :]
    for field in range(FIELDS):
        begin = field % 2 * FOLD
        first[MAIN + field] = partner[MAIN + field // 2, begin : begin + EDGE, :]
        last[MAIN + field] = partner[MAIN + field // 2, begin + EDGE : begin + FOLD, :]


def steps(
    side, injection, adjoint, lon_wind, lat_wind, mixing, partner, near, lon_same, lon_cross,
    own_below, own_above, below, above, prior,
    kept, returned, weights,
    field_ref, lon_ref, lat_ref, kab_ref, inv_ref, cp_ref, red_ref, inj_ref,
):
    refs = (adjoint, lon_wind, lat_wind, mixing)
    k = side[0]
    mine = half_at(k)
    rows = slice(0, ROWS)
    low = slice(0, EDGE)
    mid = slice(EDGE, EDGE + ROWS)
    top = slice(EDGE + ROWS, TALL)
    main = slice(0, HALF)
    wing = slice(HALF, WIDE)

    west = k == 0
    lane = lax.broadcasted_iota(jnp.int32, (FOLD, HALF), 1) < HALF // 2

    def turned(x, shift):
        return pltpu.roll(x, shift % HALF, 1) if shift % HALF else x

    def rim(pair, begin):
        ahead, behind = pair
        return jnp.where(lane[: ahead.shape[0]], turned(ahead, -begin), turned(behind, -begin - EDGE))

    def ends(inside, outside):
        return jnp.where(west, inside, outside), jnp.where(west, outside, inside)

    for group in range(2):
        base = (k if group == 0 else 1 - k) * HERE
        under, over = (own_below, own_above) if group == 0 else (below, above)
        for field in range(FIELDS):
            if group == 0:
                inside = (own_below[MAIN + field], near[field], own_above[MAIN + field])
            else:
                begin = field % 2 * FOLD
                inside = (below[MAIN + field], partner[MAIN + field // 2, begin : begin + FOLD, :], above[MAIN + field])
            at = MAIN + (1 + group) * FIELDS + field
            outside = (own_below[at], (lon_same, lon_cross)[group][field], own_above[at])
            south_rim, middle_rim, north_rim = (ends(*pair) for pair in zip(inside, outside))
            for level in range(HERE):
                at = field * HERE + level
                where = base + level
                if field < TRACERS:
                    target = field_ref.at[field, where]
                else:
                    target = (lon_ref, lat_ref, kab_ref)[field - TRACERS].at[where]
                target[low, main] = under[at]
                target[top, main] = over[at]
                if group == 0:
                    target[mid, main] = own_plane(refs, field, level, rows, mine)
                else:
                    target[mid, main] = partner[at]
                target[low, wing] = rim(south_rim, EDGE * (HERE + level))
                target[EDGE : EDGE + FOLD, wing] = rim(middle_rim, EDGE * level)
                target[EDGE + FOLD : EDGE + ROWS, wing] = rim(middle_rim, EDGE * (HERE + level))
                target[top, wing] = rim(north_rim, EDGE * level)
    for tracer in range(TRACERS):
        for level in range(HERE):
            row = tracer * HERE + level
            inj_ref[tracer, pl.ds(k * HERE + level, 1)] = jnp.broadcast_to(
                injection[tracer : tracer + 1, level : level + 1][None], (1, 8, HALF)
            )
            inj_ref[tracer, pl.ds((1 - k) * HERE + level, 1)] = jnp.broadcast_to(
                partner[PLANES - 1, row : row + 1, :][None], (1, 8, HALF)
            )
    kab_ref[LEVELS - 1] = jnp.zeros((TALL, WIDE), jnp.float32)

    def pivots(tile, _):
        at = pl.ds(pl.multiple_of(tile * 8, 8), 8)
        carried = jnp.zeros((8, WIDE), jnp.float32)
        kbelow = jnp.zeros((8, WIDE), jnp.float32)
        for level in range(LEVELS):
            kabove = kab_ref[level, at, :]
            inverse = 1.0 / (1.0 + kabove + kbelow * (1.0 + carried))
            carried = -kabove * inverse
            inv_ref[level, at, :] = inverse
            cp_ref[level, at, :] = carried
            kbelow = kabove
        return 0

    lax.fori_loop(0, TALL // 8, pivots, 0)

    def one_step(step, _):
        def solve(tile, _):
            at = pl.ds(pl.multiple_of(tile * 8, 8), 8)
            carried = [jnp.zeros((8, WIDE), jnp.float32) for _ in range(TRACERS)]
            for level in range(LEVELS):
                inverse = inv_ref[level, at, :]
                if level:
                    kbelow = kab_ref[level - 1, at, :]
                for tracer in range(TRACERS):
                    rhs = field_ref[tracer, level, at, :]
                    if level:
                        rhs = rhs + kbelow * carried[tracer]
                    carried[tracer] = rhs * inverse
                    red_ref[tracer, level] = carried[tracer]
            for tracer in range(TRACERS):
                field_ref[tracer, LEVELS - 1, at, :] = carried[tracer]
            for level in reversed(range(LEVELS - 1)):
                cprime = cp_ref[level, at, :]
                for tracer in range(TRACERS):
                    carried[tracer] = red_ref[tracer, level] - cprime * carried[tracer]
                    field_ref[tracer, level, at, :] = carried[tracer]
            return 0

        lax.fori_loop(0, TALL // 8, solve, 0)

        def weigh(tile, _):
            at = pl.ds(pl.multiple_of(tile * 8 + EDGE, 8), 8)
            to = pl.ds(pl.multiple_of(tile * 8, 8), 8)
            for tracer in range(TRACERS):
                total = jnp.zeros((8, HALF), jnp.float32)
                for level in range(LEVELS):
                    total = total + inj_ref[tracer, level] * field_ref[tracer, level, at, main]
                weights[step * TRACERS + tracer, to, :] = total
            return 0

        lax.fori_loop(0, ROWS // 8, weigh, 0)

        def advect(level, _):
            lon = lon_ref[level]
            lat = lat_ref[level]
            east = lon > 0.0
            north = lat > 0.0
            lon = jnp.abs(lon)
            lat = jnp.abs(lat)
            centre = 1.0 - lon - lat
            for tracer in range(TRACERS):
                cells = field_ref[tracer, level]
                along = jnp.where(east, pltpu.roll(cells, WIDE - 1, 1), pltpu.roll(cells, 1, 1))
                across = jnp.where(north, pltpu.roll(cells, TALL - 1, 0), pltpu.roll(cells, 1, 0))
                field_ref[tracer, level] = centre * cells + lon * along + lat * across
            return 0

        def settle(level, _):
            around = slice(0, TALL)
            lon = lon_ref[level, mid, main]
            lat = lat_ref[level, mid, main]
            for tracer in range(TRACERS):
                cells = field_ref[tracer, level, mid, :]
                column = field_ref[tracer, level, around, main]
                along = jnp.where(
                    lon > 0.0, pltpu.roll(cells, WIDE - 1, 1)[:, main], pltpu.roll(cells, 1, 1)[:, main]
                )
                across = jnp.where(lat > 0.0, pltpu.roll(column, TALL - 1, 0)[mid], pltpu.roll(column, 1, 0)[mid])
                here = cells[:, main]
                field_ref[tracer, level, mid, main] = (
                    (1.0 - jnp.abs(lon) - jnp.abs(lat)) * here + jnp.abs(lon) * along + jnp.abs(lat) * across
                )
            return 0

        @pl.when(step < STEPS - 1)
        def _():
            lax.fori_loop(0, LEVELS, advect, 0)

        @pl.when(step == STEPS - 1)
        def _():
            lax.fori_loop(0, LEVELS, settle, 0)

        return 0

    lax.fori_loop(0, STEPS, one_step, 0)

    for tracer in range(TRACERS):
        flux = prior[tracer, :, mine].astype(jnp.float32)
        for step in range(STEPS):
            weights[step * TRACERS + tracer] = weights[step * TRACERS + tracer] * flux
        for level in range(HERE):
            kept[tracer, level] = field_ref[tracer, k * HERE + level, mid, main]
            returned[tracer, level] = field_ref[tracer, (1 - k) * HERE + level, mid, main]


def regions(side, weights, ids, sums, onehot, coarse, fine):
    mine = half_at(side[0])
    count = STEPS * TRACERS
    which = lax.broadcasted_iota(jnp.int32, (HI, HALF), 0)
    blank = jnp.zeros((SLOT - count, HALF), jnp.float32)
    nothing = jnp.zeros((SLOT, HALF), jnp.float32)
    for row in range(ROWS):
        at = slice(row * HALF, (row + 1) * HALF)
        region = ids[row : row + 1, mine]
        onehot[:, at] = jnp.where(which == region // LO, 1.0, 0.0).astype(jnp.bfloat16)
        value = jnp.concatenate([weights[:, row, :], blank], axis=0)
        big = value.astype(jnp.bfloat16).astype(jnp.float32)
        small = value - big
        for low in range(LO):
            here = region % LO == low
            to = slice(low * SLOT, (low + 1) * SLOT)
            coarse[to, at] = jnp.where(here, big, nothing).astype(jnp.bfloat16)
            fine[to, at] = jnp.where(here, small, nothing).astype(jnp.bfloat16)
    dims = (((1,), (1,)), ((), ()))
    total = lax.dot_general(onehot[...], coarse[...], dims, preferred_element_type=jnp.float32)
    total = total + lax.dot_general(onehot[...], fine[...], dims, preferred_element_type=jnp.float32)
    sums[pl.ds(0, HI, stride=2)] = total[:, :HALF]
    sums[pl.ds(1, HI, stride=2)] = total[:, HALF:]


def join(side, kept, received, out):
    k = side[0]
    for tracer in range(TRACERS):
        for level in range(HERE):
            out[tracer, level, :, half_at(k)] = kept[tracer, level]
            out[tracer, level, :, half_at(1 - k)] = received[tracer, level]


def body(adjoint, courant_lon, courant_lat, mixing, injection, prior_flux, region_ids):
    lon_count = lax.axis_size("lon")
    lat_count = lax.axis_size("lat")
    side = lax.axis_index("lev").astype(jnp.int32).reshape(1)
    raw = tuple(
        pltpu.with_memory_space_constraint(x, pltpu.HBM) for x in (adjoint, courant_lon, courant_lat, mixing)
    )
    own = tuple(hold(x) for x in (adjoint, courant_lon, courant_lat, mixing))
    injection = hold(injection)

    edge_inner, edge_cross, edge_same, edge_near = call(
        pack_edges, tuple(near(FIELDS, FOLD, HALF) for _ in range(4)), (side, *raw), 1
    )
    same = []
    cross = []
    for i in range(lon_count):
        after = (i + 1) % lon_count
        same += [(2 * i, 2 * after), (2 * after + 1, 2 * i + 1)]
        cross += [(2 * i + 1, 2 * after), (2 * after, 2 * i + 1)]
    north = [(j, j + 1) for j in range(lat_count - 1)]
    south = [(j + 1, j) for j in range(lat_count - 1)]
    lon_cross = permute(edge_cross, ("lon", "lev"), cross)
    lon_same = permute(edge_same, ("lon", "lev"), same)

    to_partner = call(pack_main, near(PLANES, ROWS, HALF), (side, injection, *own, edge_inner), 1, work=100000000)
    partner = permute(to_partner, "lev", [(0, 1), (1, 0)])

    strip = MAIN + 3 * FIELDS
    first, last = call(
        own_strips,
        (near(strip, EDGE, HALF), near(strip, EDGE, HALF)),
        (side, *own, edge_near, lon_same, lon_cross),
        1,
        work=10000000000,
    )
    own_below = permute(last, "lat", north)
    own_above = permute(first, "lat", south)

    strip = MAIN + FIELDS
    first, last = call(
        strips,
        (near(strip, EDGE, HALF), near(strip, EDGE, HALF)),
        (partner, own_below, own_above),
        0,
    )
    below = permute(last, "lat", north)
    above = permute(first, "lat", south)

    block = (LEVELS, TALL, WIDE)
    kept, returned, weights = call(
        steps,
        (
            near(TRACERS, HERE, ROWS, HALF),
            near(TRACERS, HERE, ROWS, HALF),
            near(STEPS * TRACERS, ROWS, HALF),
        ),
        (
            side, injection, *own, partner, edge_near, lon_same, lon_cross,
            own_below, own_above, below, above, hold(prior_flux),
        ),
        1,
        [
            pltpu.VMEM((TRACERS, *block), jnp.float32),
            pltpu.VMEM(block, jnp.float32),
            pltpu.VMEM(block, jnp.float32),
            pltpu.VMEM(block, jnp.float32),
            pltpu.VMEM(block, jnp.float32),
            pltpu.VMEM(block, jnp.float32),
            pltpu.VMEM((TRACERS, LEVELS, 8, WIDE), jnp.float32),
            pltpu.VMEM((TRACERS, LEVELS, 8, HALF), jnp.float32),
        ],
        24,
    )
    received = permute(returned, "lev", [(0, 1), (1, 0)])
    sums = call(
        regions,
        near(2 * HI, HALF),
        (side, weights, region_ids),
        1,
        [pltpu.VMEM((HI, ROWS * HALF), jnp.bfloat16) for _ in range(3)],
        12,
    )
    pieces = lax.all_to_all(sums, ("lon", "lat", "lev"), 0, 0, tiled=True)
    region_grad = jnp.sum(pieces, axis=0).reshape(-1, SLOT)[:, : STEPS * TRACERS]
    adjoint_out = call(join, f32(*adjoint.shape), (side, kept, received), 1)
    return (adjoint_out, region_grad)


def solution(mesh):
    placed = (
        P(None, "lev", "lat", "lon"),
        P("lev", "lat", "lon"),
        P("lev", "lat", "lon"),
        P("lev", "lat", "lon"),
        P(None, "lev"),
        P(None, "lat", "lon"),
        P("lat", "lon"),
    )
    return jax.shard_map(
        body,
        mesh=mesh,
        in_specs=placed,
        out_specs=(P(None, "lev", "lat", "lon"), P(("lon", "lat", "lev"), None)),
        check_vma=False,
    )
```

```python
import jax
import jax.numpy as jnp
from jax import lax
from jax.experimental import pallas as pl
from jax.experimental.pallas import tpu as pltpu
from jax.sharding import PartitionSpec as P

STEPS = 6
TRACERS = 4
FIELDS = TRACERS + 3
HERE = 8
LEVELS = 16
ROWS = 32
HALF = 128
EDGE = 8
TALL = ROWS + 2 * EDGE
WIDE = 2 * HALF
MAIN = FIELDS * HERE
FOLD = 2 * EDGE
PLANES = MAIN + (FIELDS + 1) // 2 + 1
HI = 256
LO = 8
SLOT = 32

VMEM = pl.BlockSpec(memory_space=pltpu.VMEM)
SMEM = pl.BlockSpec(memory_space=pltpu.SMEM)
MIB = 1024 * 1024


def call(kernel, out_shape, operands, scalars, scratch=(), limit=8):
    specs = [SMEM] * scalars + [VMEM] * (len(operands) - scalars)
    many = isinstance(out_shape, (tuple, list))
    return pl.pallas_call(
        kernel,
        out_shape=out_shape,
        in_specs=specs,
        out_specs=tuple(VMEM for _ in out_shape) if many else VMEM,
        scratch_shapes=list(scratch),
        compiler_params=pltpu.CompilerParams(vmem_limit_bytes=limit * MIB),
        name=kernel.__name__,
    )(*operands)


def f32(*shape):
    return jax.ShapeDtypeStruct(shape, jnp.float32)


def near(*shape):
    return pltpu.VMEM(shape, jnp.float32)


def hold(x):
    return pltpu.with_memory_space_constraint(x, pltpu.VMEM)


def permute(x, axes, pairs):
    return hold(lax.ppermute(x, axes, pairs))


def half_at(which):
    return pl.ds(pl.multiple_of(which * HALF, HALF), HALF)


def own_plane(refs, field, level, rows, lanes):
    adjoint, lon_wind, lat_wind, mixing = refs
    if field < TRACERS:
        return adjoint[field, level, rows, lanes]
    ref = (lon_wind, lat_wind, mixing)[field - TRACERS]
    return ref[level, rows, lanes].astype(jnp.float32)


def pack_edges(side, adjoint, lon_wind, lat_wind, mixing, inner, cross, same, near):
    refs = (adjoint, lon_wind, lat_wind, mixing)
    k = side[0]
    mine = half_at(k)
    other = half_at(1 - k)
    slot = lax.broadcasted_iota(jnp.int32, (FOLD, HALF), 1) // EDGE
    upper = slice(0, FOLD)
    lower = slice(FOLD, ROWS)
    west = k == 0

    def packed(planes, begin):
        out = jnp.zeros((FOLD, HALF), jnp.float32)
        for level, plane in enumerate(planes):
            for rows, to in ((upper, level), (lower, HERE + level)):
                shift = (EDGE * to - begin) % HALF
                moved = pltpu.roll(plane[rows], shift, 1) if shift else plane[rows]
                out = jnp.where(slot == to, moved, out)
        return out

    for field in range(FIELDS):
        planes = [own_plane(refs, field, level, slice(0, ROWS), mine) for level in range(HERE)]
        low = packed(planes, 0)
        high = packed(planes, HALF - EDGE)
        inner[field] = jnp.where(west, high, low)
        cross[field] = jnp.where(west, low, high)
        planes = [own_plane(refs, field, level, slice(0, ROWS), other) for level in range(HERE)]
        low = packed(planes, 0)
        high = packed(planes, HALF - EDGE)
        same[field] = jnp.where(west, high, low)
        near[field] = jnp.where(west, low, high)


def pack_main(side, injection, adjoint, lon_wind, lat_wind, mixing, inner, near, to_partner, first, last):
    refs = (adjoint, lon_wind, lat_wind, mixing)
    mine = half_at(side[0])
    other = half_at(1 - side[0])
    for field in range(FIELDS):
        for level in range(HERE):
            at = field * HERE + level
            to_partner[at] = own_plane(refs, field, level, slice(0, ROWS), other)
            plane = own_plane(refs, field, level, slice(0, ROWS), mine)
            first[at] = plane[:EDGE]
            last[at] = plane[ROWS - EDGE :]
        to_partner[MAIN + field // 2, pl.ds(field % 2 * FOLD, FOLD), :] = inner[field]
        first[MAIN + field] = near[field, :EDGE]
        last[MAIN + field] = near[field, EDGE:]
    for tracer in range(TRACERS):
        for level in range(HERE):
            row = tracer * HERE + level
            to_partner[PLANES - 1, row : row + 1, :] = jnp.broadcast_to(
                injection[tracer : tracer + 1, level : level + 1], (1, HALF)
            )


def strips(partner, lon_same, lon_cross, own_below, own_above, first, last):
    first[0:MAIN] = partner[0:MAIN, 0:EDGE, :]
    last[0:MAIN] = partner[0:MAIN, ROWS - EDGE : ROWS, :]
    for field in range(FIELDS):
        begin = field % 2 * FOLD
        first[MAIN + field] = partner[MAIN + field // 2, begin : begin + EDGE, :]
        last[MAIN + field] = partner[MAIN + field // 2, begin + EDGE : begin + FOLD, :]
    for group, rims in enumerate((lon_same, lon_cross)):
        at = slice(MAIN + (1 + group) * FIELDS, MAIN + (2 + group) * FIELDS)
        first[at] = rims[:, :EDGE, :]
        last[at] = rims[:, EDGE:, :]


def steps(
    side, injection, adjoint, lon_wind, lat_wind, mixing, partner, near, lon_same, lon_cross,
    own_below, own_above, below, above, prior,
    kept, returned, weights,
    field_ref, lon_ref, lat_ref, kab_ref, inv_ref, cp_ref, red_ref, inj_ref,
):
    refs = (adjoint, lon_wind, lat_wind, mixing)
    k = side[0]
    mine = half_at(k)
    rows = slice(0, ROWS)
    low = slice(0, EDGE)
    mid = slice(EDGE, EDGE + ROWS)
    top = slice(EDGE + ROWS, TALL)
    main = slice(0, HALF)
    wing = slice(HALF, WIDE)

    west = k == 0
    lane = lax.broadcasted_iota(jnp.int32, (FOLD, HALF), 1) < HALF // 2

    def turned(x, shift):
        return pltpu.roll(x, shift % HALF, 1) if shift % HALF else x

    def rim(pair, begin):
        ahead, behind = pair
        return jnp.where(lane[: ahead.shape[0]], turned(ahead, -begin), turned(behind, -begin - EDGE))

    def ends(inside, outside):
        return jnp.where(west, inside, outside), jnp.where(west, outside, inside)

    for group in range(2):
        base = (k if group == 0 else 1 - k) * HERE
        under, over = (own_below, own_above) if group == 0 else (below, above)
        for field in range(FIELDS):
            if group == 0:
                inside = (own_below[MAIN + field], near[field], own_above[MAIN + field])
            else:
                begin = field % 2 * FOLD
                inside = (below[MAIN + field], partner[MAIN + field // 2, begin : begin + FOLD, :], above[MAIN + field])
            at = MAIN + (1 + group) * FIELDS + field
            outside = (below[at], (lon_same, lon_cross)[group][field], above[at])
            south_rim, middle_rim, north_rim = (ends(*pair) for pair in zip(inside, outside))
            for level in range(HERE):
                at = field * HERE + level
                where = base + level
                if field < TRACERS:
                    target = field_ref.at[field, where]
                else:
                    target = (lon_ref, lat_ref, kab_ref)[field - TRACERS].at[where]
                target[low, main] = under[at]
                target[top, main] = over[at]
                if group == 0:
                    target[mid, main] = own_plane(refs, field, level, rows, mine)
                else:
                    target[mid, main] = partner[at]
                target[low, wing] = rim(south_rim, EDGE * (HERE + level))
                target[EDGE : EDGE + FOLD, wing] = rim(middle_rim, EDGE * level)
                target[EDGE + FOLD : EDGE + ROWS, wing] = rim(middle_rim, EDGE * (HERE + level))
                target[top, wing] = rim(north_rim, EDGE * level)
    for tracer in range(TRACERS):
        for level in range(HERE):
            row = tracer * HERE + level
            inj_ref[tracer, pl.ds(k * HERE + level, 1)] = jnp.broadcast_to(
                injection[tracer : tracer + 1, level : level + 1][None], (1, 8, HALF)
            )
            inj_ref[tracer, pl.ds((1 - k) * HERE + level, 1)] = jnp.broadcast_to(
                partner[PLANES - 1, row : row + 1, :][None], (1, 8, HALF)
            )
    kab_ref[LEVELS - 1] = jnp.zeros((TALL, WIDE), jnp.float32)

    def pivots(tile, _):
        at = pl.ds(pl.multiple_of(tile * 8, 8), 8)
        carried = jnp.zeros((8, WIDE), jnp.float32)
        kbelow = jnp.zeros((8, WIDE), jnp.float32)
        for level in range(LEVELS):
            kabove = kab_ref[level, at, :]
            inverse = 1.0 / (1.0 + kabove + kbelow * (1.0 + carried))
            carried = -kabove * inverse
            inv_ref[level, at, :] = inverse
            cp_ref[level, at, :] = carried
            kbelow = kabove
        return 0

    lax.fori_loop(0, TALL // 8, pivots, 0)

    def one_step(step, _):
        def solve(tile, _):
            at = pl.ds(pl.multiple_of(tile * 8, 8), 8)
            carried = [jnp.zeros((8, WIDE), jnp.float32) for _ in range(TRACERS)]
            for level in range(LEVELS):
                inverse = inv_ref[level, at, :]
                if level:
                    kbelow = kab_ref[level - 1, at, :]
                for tracer in range(TRACERS):
                    rhs = field_ref[tracer, level, at, :]
                    if level:
                        rhs = rhs + kbelow * carried[tracer]
                    carried[tracer] = rhs * inverse
                    red_ref[tracer, level] = carried[tracer]
            for tracer in range(TRACERS):
                field_ref[tracer, LEVELS - 1, at, :] = carried[tracer]
            for level in reversed(range(LEVELS - 1)):
                cprime = cp_ref[level, at, :]
                for tracer in range(TRACERS):
                    carried[tracer] = red_ref[tracer, level] - cprime * carried[tracer]
                    field_ref[tracer, level, at, :] = carried[tracer]
            return 0

        lax.fori_loop(0, TALL // 8, solve, 0)

        def weigh(tile, _):
            at = pl.ds(pl.multiple_of(tile * 8 + EDGE, 8), 8)
            to = pl.ds(pl.multiple_of(tile * 8, 8), 8)
            for tracer in range(TRACERS):
                total = jnp.zeros((8, HALF), jnp.float32)
                for level in range(LEVELS):
                    total = total + inj_ref[tracer, level] * field_ref[tracer, level, at, main]
                weights[step * TRACERS + tracer, to, :] = total
            return 0

        lax.fori_loop(0, ROWS // 8, weigh, 0)

        def advect(level, _):
            lon = lon_ref[level]
            lat = lat_ref[level]
            east = lon > 0.0
            north = lat > 0.0
            lon = jnp.abs(lon)
            lat = jnp.abs(lat)
            centre = 1.0 - lon - lat
            for tracer in range(TRACERS):
                cells = field_ref[tracer, level]
                along = jnp.where(east, pltpu.roll(cells, WIDE - 1, 1), pltpu.roll(cells, 1, 1))
                across = jnp.where(north, pltpu.roll(cells, TALL - 1, 0), pltpu.roll(cells, 1, 0))
                field_ref[tracer, level] = centre * cells + lon * along + lat * across
            return 0

        def settle(level, _):
            around = slice(0, TALL)
            lon = lon_ref[level, mid, main]
            lat = lat_ref[level, mid, main]
            for tracer in range(TRACERS):
                cells = field_ref[tracer, level, mid, :]
                column = field_ref[tracer, level, around, main]
                along = jnp.where(
                    lon > 0.0, pltpu.roll(cells, WIDE - 1, 1)[:, main], pltpu.roll(cells, 1, 1)[:, main]
                )
                across = jnp.where(lat > 0.0, pltpu.roll(column, TALL - 1, 0)[mid], pltpu.roll(column, 1, 0)[mid])
                here = cells[:, main]
                field_ref[tracer, level, mid, main] = (
                    (1.0 - jnp.abs(lon) - jnp.abs(lat)) * here + jnp.abs(lon) * along + jnp.abs(lat) * across
                )
            return 0

        @pl.when(step < STEPS - 1)
        def _():
            lax.fori_loop(0, LEVELS, advect, 0)

        @pl.when(step == STEPS - 1)
        def _():
            lax.fori_loop(0, LEVELS, settle, 0)

        return 0

    lax.fori_loop(0, STEPS, one_step, 0)

    for tracer in range(TRACERS):
        flux = prior[tracer, :, mine].astype(jnp.float32)
        for step in range(STEPS):
            weights[step * TRACERS + tracer] = weights[step * TRACERS + tracer] * flux
        for level in range(HERE):
            kept[tracer, level] = field_ref[tracer, k * HERE + level, mid, main]
            returned[tracer, level] = field_ref[tracer, (1 - k) * HERE + level, mid, main]


def regions(side, weights, ids, sums, onehot, coarse, fine):
    mine = half_at(side[0])
    count = STEPS * TRACERS
    which = lax.broadcasted_iota(jnp.int32, (HI, HALF), 0)
    blank = jnp.zeros((SLOT - count, HALF), jnp.float32)
    nothing = jnp.zeros((SLOT, HALF), jnp.float32)
    for row in range(ROWS):
        at = slice(row * HALF, (row + 1) * HALF)
        region = ids[row : row + 1, mine]
        onehot[:, at] = jnp.where(which == region // LO, 1.0, 0.0).astype(jnp.bfloat16)
        value = jnp.concatenate([weights[:, row, :], blank], axis=0)
        big = value.astype(jnp.bfloat16).astype(jnp.float32)
        small = value - big
        for low in range(LO):
            here = region % LO == low
            to = slice(low * SLOT, (low + 1) * SLOT)
            coarse[to, at] = jnp.where(here, big, nothing).astype(jnp.bfloat16)
            fine[to, at] = jnp.where(here, small, nothing).astype(jnp.bfloat16)
    dims = (((1,), (1,)), ((), ()))
    total = lax.dot_general(onehot[...], coarse[...], dims, preferred_element_type=jnp.float32)
    total = total + lax.dot_general(onehot[...], fine[...], dims, preferred_element_type=jnp.float32)
    sums[pl.ds(0, HI, stride=2)] = total[:, :HALF]
    sums[pl.ds(1, HI, stride=2)] = total[:, HALF:]


def join(side, kept, received, out):
    k = side[0]
    for tracer in range(TRACERS):
        for level in range(HERE):
            out[tracer, level, :, half_at(k)] = kept[tracer, level]
            out[tracer, level, :, half_at(1 - k)] = received[tracer, level]


def body(adjoint, courant_lon, courant_lat, mixing, injection, prior_flux, region_ids):
    lon_count = lax.axis_size("lon")
    lat_count = lax.axis_size("lat")
    side = lax.axis_index("lev").astype(jnp.int32).reshape(1)
    raw = tuple(
        pltpu.with_memory_space_constraint(x, pltpu.HBM) for x in (adjoint, courant_lon, courant_lat, mixing)
    )
    own = tuple(hold(x) for x in (adjoint, courant_lon, courant_lat, mixing))
    injection = hold(injection)

    edge_inner, edge_cross, edge_same, edge_near = call(
        pack_edges, tuple(near(FIELDS, FOLD, HALF) for _ in range(4)), (side, *raw), 1
    )
    same = []
    cross = []
    for i in range(lon_count):
        after = (i + 1) % lon_count
        same += [(2 * i, 2 * after), (2 * after + 1, 2 * i + 1)]
        cross += [(2 * i + 1, 2 * after), (2 * after, 2 * i + 1)]
    north = [(j, j + 1) for j in range(lat_count - 1)]
    south = [(j + 1, j) for j in range(lat_count - 1)]
    lon_cross = permute(edge_cross, ("lon", "lev"), cross)
    lon_same = permute(edge_same, ("lon", "lev"), same)

    strip = MAIN + FIELDS
    to_partner, first, last = call(
        pack_main,
        (near(PLANES, ROWS, HALF), near(strip, EDGE, HALF), near(strip, EDGE, HALF)),
        (side, injection, *own, edge_inner, edge_near),
        1,
    )
    partner = permute(to_partner, "lev", [(0, 1), (1, 0)])
    own_below = permute(last, "lat", north)
    own_above = permute(first, "lat", south)

    strip = MAIN + 3 * FIELDS
    first, last = call(
        strips,
        (near(strip, EDGE, HALF), near(strip, EDGE, HALF)),
        (partner, lon_same, lon_cross, own_below, own_above),
        0,
    )
    below = permute(last, "lat", north)
    above = permute(first, "lat", south)

    block = (LEVELS, TALL, WIDE)
    kept, returned, weights = call(
        steps,
        (
            near(TRACERS, HERE, ROWS, HALF),
            near(TRACERS, HERE, ROWS, HALF),
            near(STEPS * TRACERS, ROWS, HALF),
        ),
        (
            side, injection, *own, partner, edge_near, lon_same, lon_cross,
            own_below, own_above, below, above, hold(prior_flux),
        ),
        1,
        [
            pltpu.VMEM((TRACERS, *block), jnp.float32),
            pltpu.VMEM(block, jnp.float32),
            pltpu.VMEM(block, jnp.float32),
            pltpu.VMEM(block, jnp.float32),
            pltpu.VMEM(block, jnp.float32),
            pltpu.VMEM(block, jnp.float32),
            pltpu.VMEM((TRACERS, LEVELS, 8, WIDE), jnp.float32),
            pltpu.VMEM((TRACERS, LEVELS, 8, HALF), jnp.float32),
        ],
        24,
    )
    received = permute(returned, "lev", [(0, 1), (1, 0)])
    sums = call(
        regions,
        near(2 * HI, HALF),
        (side, weights, region_ids),
        1,
        [pltpu.VMEM((HI, ROWS * HALF), jnp.bfloat16) for _ in range(3)],
        12,
    )
    pieces = lax.all_to_all(sums, ("lon", "lat", "lev"), 0, 0, tiled=True)
    region_grad = jnp.sum(pieces, axis=0).reshape(-1, SLOT)[:, : STEPS * TRACERS]
    adjoint_out = call(join, f32(*adjoint.shape), (side, kept, received), 1)
    return (adjoint_out, region_grad)


def solution(mesh):
    placed = (
        P(None, "lev", "lat", "lon"),
        P("lev", "lat", "lon"),
        P("lev", "lat", "lon"),
        P("lev", "lat", "lon"),
        P(None, "lev"),
        P(None, "lat", "lon"),
        P("lat", "lon"),
    )
    return jax.shard_map(
        body,
        mesh=mesh,
        in_specs=placed,
        out_specs=(P(None, "lev", "lat", "lon"), P(("lon", "lat", "lev"), None)),
        check_vma=False,
    )
```

```python
import jax
import jax.numpy as jnp
from jax import lax
from jax.experimental import pallas as pl
from jax.experimental.pallas import tpu as pltpu
from jax.sharding import PartitionSpec as P

STEPS = 6
TRACERS = 4
FIELDS = TRACERS + 3
HERE = 8
LEVELS = 16
ROWS = 32
HALF = 128
EDGE = 8
TALL = ROWS + 2 * EDGE
WIDE = 2 * HALF
MAIN = FIELDS * HERE
FOLD = 2 * EDGE
PLANES = MAIN + (FIELDS + 1) // 2 + 1
HI = 256
LO = 8
SLOT = 32

VMEM = pl.BlockSpec(memory_space=pltpu.VMEM)
SMEM = pl.BlockSpec(memory_space=pltpu.SMEM)
MIB = 1024 * 1024


def call(kernel, out_shape, operands, scalars, scratch=(), limit=8, alias=None):
    specs = [SMEM] * scalars + [VMEM] * (len(operands) - scalars)
    many = isinstance(out_shape, (tuple, list))
    return pl.pallas_call(
        kernel,
        out_shape=out_shape,
        in_specs=specs,
        out_specs=tuple(VMEM for _ in out_shape) if many else VMEM,
        scratch_shapes=list(scratch),
        compiler_params=pltpu.CompilerParams(vmem_limit_bytes=limit * MIB),
        name=kernel.__name__,
        input_output_aliases=alias or {},
    )(*operands)


def f32(*shape):
    return jax.ShapeDtypeStruct(shape, jnp.float32)


def near(*shape):
    return pltpu.VMEM(shape, jnp.float32)


def hold(x):
    return pltpu.with_memory_space_constraint(x, pltpu.VMEM)


def permute(x, axes, pairs):
    return hold(lax.ppermute(x, axes, pairs))


def half_at(which):
    return pl.ds(pl.multiple_of(which * HALF, HALF), HALF)


def own_plane(refs, field, level, rows, lanes):
    adjoint, lon_wind, lat_wind, mixing = refs
    if field < TRACERS:
        return adjoint[field, level, rows, lanes]
    ref = (lon_wind, lat_wind, mixing)[field - TRACERS]
    return ref[level, rows, lanes].astype(jnp.float32)


def pack_edges(side, adjoint, lon_wind, lat_wind, mixing, inner, cross, same, near):
    refs = (adjoint, lon_wind, lat_wind, mixing)
    k = side[0]
    mine = half_at(k)
    other = half_at(1 - k)
    slot = lax.broadcasted_iota(jnp.int32, (FOLD, HALF), 1) // EDGE
    upper = slice(0, FOLD)
    lower = slice(FOLD, ROWS)
    west = k == 0

    def packed(planes, begin):
        out = jnp.zeros((FOLD, HALF), jnp.float32)
        for level, plane in enumerate(planes):
            for rows, to in ((upper, level), (lower, HERE + level)):
                shift = (EDGE * to - begin) % HALF
                moved = pltpu.roll(plane[rows], shift, 1) if shift else plane[rows]
                out = jnp.where(slot == to, moved, out)
        return out

    for field in range(FIELDS):
        planes = [own_plane(refs, field, level, slice(0, ROWS), mine) for level in range(HERE)]
        low = packed(planes, 0)
        high = packed(planes, HALF - EDGE)
        inner[field] = jnp.where(west, high, low)
        cross[field] = jnp.where(west, low, high)
        planes = [own_plane(refs, field, level, slice(0, ROWS), other) for level in range(HERE)]
        low = packed(planes, 0)
        high = packed(planes, HALF - EDGE)
        same[field] = jnp.where(west, high, low)
        near[field] = jnp.where(west, low, high)


def pack_main(side, injection, adjoint, lon_wind, lat_wind, mixing, inner, near, to_partner, first, last):
    refs = (adjoint, lon_wind, lat_wind, mixing)
    mine = half_at(side[0])
    other = half_at(1 - side[0])
    for field in range(FIELDS):
        for level in range(HERE):
            at = field * HERE + level
            to_partner[at] = own_plane(refs, field, level, slice(0, ROWS), other)
            plane = own_plane(refs, field, level, slice(0, ROWS), mine)
            first[at] = plane[:EDGE]
            last[at] = plane[ROWS - EDGE :]
        to_partner[MAIN + field // 2, pl.ds(field % 2 * FOLD, FOLD), :] = inner[field]
        first[MAIN + field] = near[field, :EDGE]
        last[MAIN + field] = near[field, EDGE:]
    for tracer in range(TRACERS):
        for level in range(HERE):
            row = tracer * HERE + level
            to_partner[PLANES - 1, row : row + 1, :] = jnp.broadcast_to(
                injection[tracer : tracer + 1, level : level + 1], (1, HALF)
            )


def pack(
    side, injection, adjoint, lon_wind, lat_wind, mixing, inner, cross, same, near, to_partner, first, last
):
    pack_edges(side, adjoint, lon_wind, lat_wind, mixing, inner, cross, same, near)
    pack_main(side, injection, adjoint, lon_wind, lat_wind, mixing, inner, near, to_partner, first, last)


def strips(partner, lon_same, lon_cross, own_below, own_above, first, last):
    first[0:MAIN] = partner[0:MAIN, 0:EDGE, :]
    last[0:MAIN] = partner[0:MAIN, ROWS - EDGE : ROWS, :]
    for field in range(FIELDS):
        begin = field % 2 * FOLD
        first[MAIN + field] = partner[MAIN + field // 2, begin : begin + EDGE, :]
        last[MAIN + field] = partner[MAIN + field // 2, begin + EDGE : begin + FOLD, :]
    for group, rims in enumerate((lon_same, lon_cross)):
        at = slice(MAIN + (1 + group) * FIELDS, MAIN + (2 + group) * FIELDS)
        first[at] = rims[:, :EDGE, :]
        last[at] = rims[:, EDGE:, :]


def turned(x, shift):
    return pltpu.roll(x, shift % HALF, 1) if shift % HALF else x


def rim(pair, begin):
    ahead, behind = pair
    lane = lax.broadcasted_iota(jnp.int32, ahead.shape, 1) < HALF // 2
    return jnp.where(lane, turned(ahead, -begin), turned(behind, -begin - EDGE))


def ends(k, inside, outside):
    return jnp.where(k == 0, inside, outside), jnp.where(k == 0, outside, inside)


MAIN_LANES = slice(0, HALF)
WING_LANES = slice(HALF, WIDE)


def eliminate_tile(tile, kab_ref, inv_ref, cp_ref):
    at = pl.ds(pl.multiple_of(tile * 8, 8), 8)
    carried = jnp.zeros((8, WIDE), jnp.float32)
    kbelow = jnp.zeros((8, WIDE), jnp.float32)
    for level in range(LEVELS):
        kabove = kab_ref[level, at, :]
        inverse = 1.0 / (1.0 + kabove + kbelow * (1.0 + carried))
        carried = -kabove * inverse
        inv_ref[level, at, :] = inverse
        cp_ref[level, at, :] = carried
        kbelow = kabove


def solve_tile(tile, field_ref, kab_ref, inv_ref, cp_ref, red_ref):
    at = pl.ds(pl.multiple_of(tile * 8, 8), 8)
    carried = [None] * TRACERS
    for level in range(LEVELS):
        inverse = inv_ref[level, at, :]
        if level:
            kbelow = kab_ref[level - 1, at, :]
        for tracer in range(TRACERS):
            rhs = field_ref[tracer, level, at, :]
            if level:
                rhs = rhs + kbelow * carried[tracer]
            carried[tracer] = rhs * inverse
            red_ref[tracer, level] = carried[tracer]
    for tracer in range(TRACERS):
        field_ref[tracer, LEVELS - 1, at, :] = carried[tracer]
    for level in reversed(range(LEVELS - 1)):
        cprime = cp_ref[level, at, :]
        for tracer in range(TRACERS):
            carried[tracer] = red_ref[tracer, level] - cprime * carried[tracer]
            field_ref[tracer, level, at, :] = carried[tracer]


def prepare(
    side, injection, adjoint, lon_wind, lat_wind, mixing, partner, near, lon_same, lon_cross,
    field_ref, lon_ref, lat_ref, kab_ref, inv_ref, cp_ref, inj_ref, red_ref,
):
    refs = (adjoint, lon_wind, lat_wind, mixing)
    k = side[0]
    mine = half_at(k)
    for group in range(2):
        base = (k if group == 0 else 1 - k) * HERE
        for field in range(FIELDS):
            begin = field % 2 * FOLD
            inside = near[field] if group == 0 else partner[MAIN + field // 2, begin : begin + FOLD, :]
            pair = ends(k, inside, (lon_same, lon_cross)[group][field])
            for level in range(HERE):
                where = base + level
                if field < TRACERS:
                    target = field_ref.at[field, where]
                else:
                    target = (lon_ref, lat_ref, kab_ref)[field - TRACERS].at[where]
                if group == 0:
                    plane = own_plane(refs, field, level, slice(0, ROWS), mine)
                else:
                    plane = partner[field * HERE + level]
                target[EDGE : EDGE + ROWS, MAIN_LANES] = plane
                target[EDGE : EDGE + FOLD, WING_LANES] = rim(pair, EDGE * level)
                target[EDGE + FOLD : EDGE + ROWS, WING_LANES] = rim(pair, EDGE * (HERE + level))
    for tracer in range(TRACERS):
        for level in range(HERE):
            row = tracer * HERE + level
            inj_ref[tracer, pl.ds(k * HERE + level, 1)] = jnp.broadcast_to(
                injection[tracer : tracer + 1, level : level + 1][None], (1, 8, HALF)
            )
            inj_ref[tracer, pl.ds((1 - k) * HERE + level, 1)] = jnp.broadcast_to(
                partner[PLANES - 1, row : row + 1, :][None], (1, 8, HALF)
            )
    kab_ref[LEVELS - 1] = jnp.zeros((TALL, WIDE), jnp.float32)

    def inner(tile, _):
        eliminate_tile(tile, kab_ref, inv_ref, cp_ref)
        solve_tile(tile, field_ref, kab_ref, inv_ref, cp_ref, red_ref)
        return 0

    lax.fori_loop(1, 1 + ROWS // 8, inner, 0)


def steps(
    side, own_below, own_above, below, above, prior, inj_ref,
    field_in, lon_in, lat_in, kab_in, inv_in, cp_in,
    kept, returned, weights,
    field_ref, lon_ref, lat_ref, kab_ref, inv_ref, cp_ref, red_ref,
):
    k = side[0]
    mine = half_at(k)
    mid = slice(EDGE, EDGE + ROWS)
    low = slice(0, EDGE)
    top = slice(EDGE + ROWS, TALL)
    main = MAIN_LANES
    wing = WING_LANES
    for group in range(2):
        base = (k if group == 0 else 1 - k) * HERE
        under, over = (own_below, own_above) if group == 0 else (below, above)
        for field in range(FIELDS):
            near_at = MAIN + field
            far_at = MAIN + (1 + group) * FIELDS + field
            south_rim = ends(k, under[near_at], below[far_at])
            north_rim = ends(k, over[near_at], above[far_at])
            for level in range(HERE):
                at = field * HERE + level
                where = base + level
                if field < TRACERS:
                    target = field_ref.at[field, where]
                else:
                    target = (lon_ref, lat_ref, kab_ref)[field - TRACERS].at[where]
                target[low, main] = under[at]
                target[top, main] = over[at]
                target[low, wing] = rim(south_rim, EDGE * (HERE + level))
                target[top, wing] = rim(north_rim, EDGE * level)
    kab_ref[LEVELS - 1] = jnp.zeros((TALL, WIDE), jnp.float32)
    last_tile = TALL // 8 - 1

    def outer(i, _):
        eliminate_tile(i * last_tile, kab_ref, inv_ref, cp_ref)
        return 0

    lax.fori_loop(0, 2, outer, 0)

    def one_step(step, _):
        def solve(i, _):
            tile = jnp.where(step == 0, i * last_tile, i)
            solve_tile(tile, field_ref, kab_ref, inv_ref, cp_ref, red_ref)
            return 0

        lax.fori_loop(0, jnp.where(step == 0, 2, TALL // 8), solve, 0)

        def weigh(tile, _):
            at = pl.ds(pl.multiple_of(tile * 8 + EDGE, 8), 8)
            to = pl.ds(pl.multiple_of(tile * 8, 8), 8)
            for tracer in range(TRACERS):
                total = jnp.zeros((8, HALF), jnp.float32)
                for level in range(LEVELS):
                    total = total + inj_ref[tracer, level] * field_ref[tracer, level, at, main]
                weights[step * TRACERS + tracer, to, :] = total
            return 0

        lax.fori_loop(0, ROWS // 8, weigh, 0)

        def advect(level, _):
            lon = lon_ref[level]
            lat = lat_ref[level]
            east = lon > 0.0
            north = lat > 0.0
            lon = jnp.abs(lon)
            lat = jnp.abs(lat)
            centre = 1.0 - lon - lat
            for tracer in range(TRACERS):
                cells = field_ref[tracer, level]
                along = jnp.where(east, pltpu.roll(cells, WIDE - 1, 1), pltpu.roll(cells, 1, 1))
                across = jnp.where(north, pltpu.roll(cells, TALL - 1, 0), pltpu.roll(cells, 1, 0))
                field_ref[tracer, level] = centre * cells + lon * along + lat * across
            return 0

        def settle(level, _):
            around = slice(0, TALL)
            lon = lon_ref[level, mid, main]
            lat = lat_ref[level, mid, main]
            for tracer in range(TRACERS):
                cells = field_ref[tracer, level, mid, :]
                column = field_ref[tracer, level, around, main]
                along = jnp.where(
                    lon > 0.0, pltpu.roll(cells, WIDE - 1, 1)[:, main], pltpu.roll(cells, 1, 1)[:, main]
                )
                across = jnp.where(lat > 0.0, pltpu.roll(column, TALL - 1, 0)[mid], pltpu.roll(column, 1, 0)[mid])
                here = cells[:, main]
                field_ref[tracer, level, mid, main] = (
                    (1.0 - jnp.abs(lon) - jnp.abs(lat)) * here + jnp.abs(lon) * along + jnp.abs(lat) * across
                )
            return 0

        @pl.when(step < STEPS - 1)
        def _():
            lax.fori_loop(0, LEVELS, advect, 0)

        @pl.when(step == STEPS - 1)
        def _():
            lax.fori_loop(0, LEVELS, settle, 0)

        return 0

    lax.fori_loop(0, STEPS, one_step, 0)

    for tracer in range(TRACERS):
        flux = prior[tracer, :, mine].astype(jnp.float32)
        for step in range(STEPS):
            weights[step * TRACERS + tracer] = weights[step * TRACERS + tracer] * flux
        for level in range(HERE):
            kept[tracer, level] = field_ref[tracer, k * HERE + level, mid, main]
            returned[tracer, level] = field_ref[tracer, (1 - k) * HERE + level, mid, main]


def regions(side, weights, ids, sums, onehot, coarse, fine):
    mine = half_at(side[0])
    count = STEPS * TRACERS
    which = lax.broadcasted_iota(jnp.int32, (HI, HALF), 0)
    blank = jnp.zeros((SLOT - count, HALF), jnp.float32)
    nothing = jnp.zeros((SLOT, HALF), jnp.float32)
    for row in range(ROWS):
        at = slice(row * HALF, (row + 1) * HALF)
        region = ids[row : row + 1, mine]
        onehot[:, at] = jnp.where(which == region // LO, 1.0, 0.0).astype(jnp.bfloat16)
        value = jnp.concatenate([weights[:, row, :], blank], axis=0)
        big = value.astype(jnp.bfloat16).astype(jnp.float32)
        small = value - big
        for low in range(LO):
            here = region % LO == low
            to = slice(low * SLOT, (low + 1) * SLOT)
            coarse[to, at] = jnp.where(here, big, nothing).astype(jnp.bfloat16)
            fine[to, at] = jnp.where(here, small, nothing).astype(jnp.bfloat16)
    dims = (((1,), (1,)), ((), ()))
    total = lax.dot_general(onehot[...], coarse[...], dims, preferred_element_type=jnp.float32)
    total = total + lax.dot_general(onehot[...], fine[...], dims, preferred_element_type=jnp.float32)
    sums[pl.ds(0, HI, stride=2)] = total[:, :HALF]
    sums[pl.ds(1, HI, stride=2)] = total[:, HALF:]


def join(side, kept, received, out):
    k = side[0]
    for tracer in range(TRACERS):
        for level in range(HERE):
            out[tracer, level, :, half_at(k)] = kept[tracer, level]
            out[tracer, level, :, half_at(1 - k)] = received[tracer, level]


def body(adjoint, courant_lon, courant_lat, mixing, injection, prior_flux, region_ids):
    lon_count = lax.axis_size("lon")
    lat_count = lax.axis_size("lat")
    side = lax.axis_index("lev").astype(jnp.int32).reshape(1)
    raw = tuple(
        pltpu.with_memory_space_constraint(x, pltpu.HBM) for x in (adjoint, courant_lon, courant_lat, mixing)
    )
    own = tuple(hold(x) for x in (adjoint, courant_lon, courant_lat, mixing))
    injection = hold(injection)

    strip = MAIN + FIELDS
    _, edge_cross, edge_same, edge_near, to_partner, first, last = call(
        pack,
        (
            *(near(FIELDS, FOLD, HALF) for _ in range(4)),
            near(PLANES, ROWS, HALF),
            near(strip, EDGE, HALF),
            near(strip, EDGE, HALF),
        ),
        (side, injection, *raw),
        1,
    )
    same = []
    cross = []
    for i in range(lon_count):
        after = (i + 1) % lon_count
        same += [(2 * i, 2 * after), (2 * after + 1, 2 * i + 1)]
        cross += [(2 * i + 1, 2 * after), (2 * after, 2 * i + 1)]
    north = [(j, j + 1) for j in range(lat_count - 1)]
    south = [(j + 1, j) for j in range(lat_count - 1)]
    lon_cross = permute(edge_cross, ("lon", "lev"), cross)
    lon_same = permute(edge_same, ("lon", "lev"), same)

    partner = permute(to_partner, "lev", [(0, 1), (1, 0)])
    own_below = permute(last, "lat", north)
    own_above = permute(first, "lat", south)

    strip = MAIN + 3 * FIELDS
    first, last = call(
        strips,
        (near(strip, EDGE, HALF), near(strip, EDGE, HALF)),
        (partner, lon_same, lon_cross, own_below, own_above),
        0,
    )
    below = permute(last, "lat", north)
    above = permute(first, "lat", south)

    block = (LEVELS, TALL, WIDE)
    tile = pltpu.VMEM((TRACERS, LEVELS, 8, WIDE), jnp.float32)
    arrays = (near(TRACERS, *block), *(near(*block) for _ in range(5)))
    *state, inj = call(
        prepare,
        (*arrays, near(TRACERS, LEVELS, 8, HALF)),
        (side, injection, *own, partner, edge_near, lon_same, lon_cross),
        1,
        [tile],
    )
    kept, returned, weights = call(
        steps,
        (
            near(TRACERS, HERE, ROWS, HALF),
            near(TRACERS, HERE, ROWS, HALF),
            near(STEPS * TRACERS, ROWS, HALF),
            *arrays,
        ),
        (side, own_below, own_above, below, above, hold(prior_flux), hold(inj), *(hold(x) for x in state)),
        1,
        [tile],
        8,
        {7 + i: 3 + i for i in range(6)},
    )[:3]
    received = permute(returned, "lev", [(0, 1), (1, 0)])
    sums = call(
        regions,
        near(2 * HI, HALF),
        (side, weights, region_ids),
        1,
        [pltpu.VMEM((HI, ROWS * HALF), jnp.bfloat16) for _ in range(3)],
        12,
    )
    pieces = lax.all_to_all(sums, ("lon", "lat", "lev"), 0, 0, tiled=True)
    region_grad = jnp.sum(pieces, axis=0).reshape(-1, SLOT)[:, : STEPS * TRACERS]
    adjoint_out = call(join, f32(*adjoint.shape), (side, kept, received), 1)
    return (adjoint_out, region_grad)


def solution(mesh):
    placed = (
        P(None, "lev", "lat", "lon"),
        P("lev", "lat", "lon"),
        P("lev", "lat", "lon"),
        P("lev", "lat", "lon"),
        P(None, "lev"),
        P(None, "lat", "lon"),
        P("lat", "lon"),
    )
    return jax.shard_map(
        body,
        mesh=mesh,
        in_specs=placed,
        out_specs=(P(None, "lev", "lat", "lon"), P(("lon", "lat", "lev"), None)),
        check_vma=False,
    )
```

```python
import jax
import jax.numpy as jnp
from jax import lax
from jax.experimental import pallas as pl
from jax.experimental.pallas import tpu as pltpu
from jax.sharding import PartitionSpec as P

STEPS = 6
TRACERS = 4
FIELDS = TRACERS + 3
HERE = 8
LEVELS = 16
ROWS = 32
HALF = 128
EDGE = 8
TALL = ROWS + 2 * EDGE
WIDE = 2 * HALF
MAIN = FIELDS * HERE
FOLD = 2 * EDGE
PLANES = MAIN + (FIELDS + 1) // 2 + 1
HI = 256
LO = 8
SLOT = 32

VMEM = pl.BlockSpec(memory_space=pltpu.VMEM)
SMEM = pl.BlockSpec(memory_space=pltpu.SMEM)
MIB = 1024 * 1024


def call(kernel, out_shape, operands, scalars, scratch=(), limit=8, alias=None):
    specs = [SMEM] * scalars + [VMEM] * (len(operands) - scalars)
    many = isinstance(out_shape, (tuple, list))
    return pl.pallas_call(
        kernel,
        out_shape=out_shape,
        in_specs=specs,
        out_specs=tuple(VMEM for _ in out_shape) if many else VMEM,
        scratch_shapes=list(scratch),
        compiler_params=pltpu.CompilerParams(vmem_limit_bytes=limit * MIB),
        name=kernel.__name__,
        input_output_aliases=alias or {},
    )(*operands)


def f32(*shape):
    return jax.ShapeDtypeStruct(shape, jnp.float32)


def near(*shape):
    return pltpu.VMEM(shape, jnp.float32)


def hold(x):
    return pltpu.with_memory_space_constraint(x, pltpu.VMEM)


def permute(x, axes, pairs):
    return hold(lax.ppermute(x, axes, pairs))


def half_at(which):
    return pl.ds(pl.multiple_of(which * HALF, HALF), HALF)


def own_plane(refs, field, level, rows, lanes):
    adjoint, lon_wind, lat_wind, mixing = refs
    if field < TRACERS:
        return adjoint[field, level, rows, lanes]
    ref = (lon_wind, lat_wind, mixing)[field - TRACERS]
    return ref[level, rows, lanes].astype(jnp.float32)


def pack_edges(side, adjoint, lon_wind, lat_wind, mixing, inner, cross, same, near):
    refs = (adjoint, lon_wind, lat_wind, mixing)
    k = side[0]
    mine = half_at(k)
    other = half_at(1 - k)
    slot = lax.broadcasted_iota(jnp.int32, (FOLD, HALF), 1) // EDGE
    upper = slice(0, FOLD)
    lower = slice(FOLD, ROWS)
    west = k == 0

    def packed(planes, begin):
        out = jnp.zeros((FOLD, HALF), jnp.float32)
        for level, plane in enumerate(planes):
            for rows, to in ((upper, level), (lower, HERE + level)):
                shift = (EDGE * to - begin) % HALF
                moved = pltpu.roll(plane[rows], shift, 1) if shift else plane[rows]
                out = jnp.where(slot == to, moved, out)
        return out

    for field in range(FIELDS):
        planes = [own_plane(refs, field, level, slice(0, ROWS), mine) for level in range(HERE)]
        low = packed(planes, 0)
        high = packed(planes, HALF - EDGE)
        inner[field] = jnp.where(west, high, low)
        cross[field] = jnp.where(west, low, high)
        planes = [own_plane(refs, field, level, slice(0, ROWS), other) for level in range(HERE)]
        low = packed(planes, 0)
        high = packed(planes, HALF - EDGE)
        same[field] = jnp.where(west, high, low)
        near[field] = jnp.where(west, low, high)


def pack_main(side, injection, adjoint, lon_wind, lat_wind, mixing, inner, near, to_partner, first, last):
    refs = (adjoint, lon_wind, lat_wind, mixing)
    mine = half_at(side[0])
    other = half_at(1 - side[0])
    for field in range(FIELDS):
        for level in range(HERE):
            at = field * HERE + level
            to_partner[at] = own_plane(refs, field, level, slice(0, ROWS), other)
            plane = own_plane(refs, field, level, slice(0, ROWS), mine)
            first[at] = plane[:EDGE]
            last[at] = plane[ROWS - EDGE :]
        to_partner[MAIN + field // 2, pl.ds(field % 2 * FOLD, FOLD), :] = inner[field]
        first[MAIN + field] = near[field, :EDGE]
        last[MAIN + field] = near[field, EDGE:]
    for tracer in range(TRACERS):
        for level in range(HERE):
            row = tracer * HERE + level
            to_partner[PLANES - 1, row : row + 1, :] = jnp.broadcast_to(
                injection[tracer : tracer + 1, level : level + 1], (1, HALF)
            )


def pack(
    side, injection, adjoint, lon_wind, lat_wind, mixing, inner, cross, same, near, to_partner, first, last
):
    pack_edges(side, adjoint, lon_wind, lat_wind, mixing, inner, cross, same, near)
    pack_main(side, injection, adjoint, lon_wind, lat_wind, mixing, inner, near, to_partner, first, last)


def strips(partner, lon_same, lon_cross, own_below, own_above, first, last):
    first[0:MAIN] = partner[0:MAIN, 0:EDGE, :]
    last[0:MAIN] = partner[0:MAIN, ROWS - EDGE : ROWS, :]
    for field in range(FIELDS):
        begin = field % 2 * FOLD
        first[MAIN + field] = partner[MAIN + field // 2, begin : begin + EDGE, :]
        last[MAIN + field] = partner[MAIN + field // 2, begin + EDGE : begin + FOLD, :]
    for group, rims in enumerate((lon_same, lon_cross)):
        at = slice(MAIN + (1 + group) * FIELDS, MAIN + (2 + group) * FIELDS)
        first[at] = rims[:, :EDGE, :]
        last[at] = rims[:, EDGE:, :]


def turned(x, shift):
    return pltpu.roll(x, shift % HALF, 1) if shift % HALF else x


def rim(pair, begin):
    ahead, behind = pair
    lane = lax.broadcasted_iota(jnp.int32, ahead.shape, 1) < HALF // 2
    return jnp.where(lane, turned(ahead, -begin), turned(behind, -begin - EDGE))


def ends(k, inside, outside):
    return jnp.where(k == 0, inside, outside), jnp.where(k == 0, outside, inside)


MAIN_LANES = slice(0, HALF)
WING_LANES = slice(HALF, WIDE)


def eliminate_tile(tile, kab_ref, inv_ref, cp_ref):
    at = pl.ds(pl.multiple_of(tile * 8, 8), 8)
    carried = jnp.zeros((8, WIDE), jnp.float32)
    kbelow = jnp.zeros((8, WIDE), jnp.float32)
    for level in range(LEVELS):
        kabove = kab_ref[level, at, :]
        inverse = 1.0 / (1.0 + kabove + kbelow * (1.0 + carried))
        carried = -kabove * inverse
        inv_ref[level, at, :] = inverse
        cp_ref[level, at, :] = carried
        kbelow = kabove


def solve_tile(tile, field_ref, solved_ref, kab_ref, inv_ref, cp_ref, red_ref):
    at = pl.ds(pl.multiple_of(tile * 8, 8), 8)
    carried = [None] * TRACERS
    for level in range(LEVELS):
        inverse = inv_ref[level, at, :]
        if level:
            kbelow = kab_ref[level - 1, at, :]
        for tracer in range(TRACERS):
            rhs = field_ref[tracer, level, at, :]
            if level:
                rhs = rhs + kbelow * carried[tracer]
            carried[tracer] = rhs * inverse
            red_ref[tracer, level] = carried[tracer]
    for tracer in range(TRACERS):
        solved_ref[tracer, LEVELS - 1, at, :] = carried[tracer]
    for level in reversed(range(LEVELS - 1)):
        cprime = cp_ref[level, at, :]
        for tracer in range(TRACERS):
            carried[tracer] = red_ref[tracer, level] - cprime * carried[tracer]
            solved_ref[tracer, level, at, :] = carried[tracer]


TILES = TALL // 8
UNROLL = 4


def rows_of(tile):
    return pl.ds(pl.multiple_of(tile * 8, 8), 8)


def advect_tile(level, tile, field_ref, solved_ref, lon_ref, lat_ref, wings):
    at = rows_of(tile)
    before = rows_of(jnp.where(tile == 0, TILES - 1, tile - 1))
    after = rows_of(jnp.where(tile == TILES - 1, 0, tile + 1))
    sides = (MAIN_LANES, WING_LANES)
    count = 2 if wings else 1
    row = lax.broadcasted_iota(jnp.int32, (8, HALF), 0)
    lane = lax.broadcasted_iota(jnp.int32, (8, HALF), 1)
    rates = []
    for side in sides[:count]:
        lon = lon_ref[level, at, side]
        lat = lat_ref[level, at, side]
        rates.append((lon > 0.0, lat > 0.0, jnp.abs(lon), jnp.abs(lat)))
    for tracer in range(TRACERS):
        cells = [solved_ref[tracer, level, at, side] for side in sides]
        for i, side in enumerate(sides[:count]):
            east, north, lon, lat = rates[i]
            here = cells[i]
            beside = cells[1 - i]
            along = jnp.where(
                east,
                pltpu.roll(jnp.where(lane == 0, beside, here), HALF - 1, 1),
                pltpu.roll(jnp.where(lane == HALF - 1, beside, here), 1, 1),
            )
            across = jnp.where(
                north,
                pltpu.roll(jnp.where(row == 0, solved_ref[tracer, level, after, side], here), 7, 0),
                pltpu.roll(jnp.where(row == 7, solved_ref[tracer, level, before, side], here), 1, 0),
            )
            field_ref[tracer, level, at, side] = here + lon * (along - here) + lat * (across - here)


def advect_tiles(count, tile_of, field_ref, solved_ref, lon_ref, lat_ref, wings=True):
    blocks = LEVELS // UNROLL

    def some(i, _):
        tile = tile_of(i // blocks)
        for level in range(UNROLL):
            advect_tile(i % blocks * UNROLL + level, tile, field_ref, solved_ref, lon_ref, lat_ref, wings)
        return 0

    lax.fori_loop(0, count * blocks, some, 0)


def prepare(
    side, injection, adjoint, lon_wind, lat_wind, mixing, partner, near, lon_same, lon_cross,
    field_ref, solved_ref, lon_ref, lat_ref, kab_ref, inv_ref, cp_ref, inj_ref, red_ref,
):
    refs = (adjoint, lon_wind, lat_wind, mixing)
    k = side[0]
    mine = half_at(k)
    for group in range(2):
        base = (k if group == 0 else 1 - k) * HERE
        for field in range(FIELDS):
            begin = field % 2 * FOLD
            inside = near[field] if group == 0 else partner[MAIN + field // 2, begin : begin + FOLD, :]
            pair = ends(k, inside, (lon_same, lon_cross)[group][field])
            for level in range(HERE):
                where = base + level
                if field < TRACERS:
                    target = field_ref.at[field, where]
                else:
                    target = (lon_ref, lat_ref, kab_ref)[field - TRACERS].at[where]
                if group == 0:
                    plane = own_plane(refs, field, level, slice(0, ROWS), mine)
                else:
                    plane = partner[field * HERE + level]
                target[EDGE : EDGE + ROWS, MAIN_LANES] = plane
                target[EDGE : EDGE + FOLD, WING_LANES] = rim(pair, EDGE * level)
                target[EDGE + FOLD : EDGE + ROWS, WING_LANES] = rim(pair, EDGE * (HERE + level))
    for tracer in range(TRACERS):
        for level in range(HERE):
            row = tracer * HERE + level
            inj_ref[tracer, pl.ds(k * HERE + level, 1)] = jnp.broadcast_to(
                injection[tracer : tracer + 1, level : level + 1][None], (1, 8, HALF)
            )
            inj_ref[tracer, pl.ds((1 - k) * HERE + level, 1)] = jnp.broadcast_to(
                partner[PLANES - 1, row : row + 1, :][None], (1, 8, HALF)
            )
    kab_ref[LEVELS - 1] = jnp.zeros((TALL, WIDE), jnp.float32)

    def inner(tile, _):
        eliminate_tile(tile, kab_ref, inv_ref, cp_ref)
        solve_tile(tile, field_ref, solved_ref, kab_ref, inv_ref, cp_ref, red_ref)
        return 0

    lax.fori_loop(1, 1 + ROWS // 8, inner, 0)
    advect_tiles(2, lambda i: i + 2, field_ref, solved_ref, lon_ref, lat_ref)


def steps(
    side, own_below, own_above, below, above, prior, inj_ref,
    field_in, solved_in, lon_in, lat_in, kab_in, inv_in, cp_in,
    kept, returned, weights,
    field_ref, solved_ref, lon_ref, lat_ref, kab_ref, inv_ref, cp_ref, red_ref,
):
    k = side[0]
    mine = half_at(k)
    mid = slice(EDGE, EDGE + ROWS)
    low = slice(0, EDGE)
    top = slice(EDGE + ROWS, TALL)
    main = MAIN_LANES
    wing = WING_LANES
    for group in range(2):
        base = (k if group == 0 else 1 - k) * HERE
        under, over = (own_below, own_above) if group == 0 else (below, above)
        for field in range(FIELDS):
            near_at = MAIN + field
            far_at = MAIN + (1 + group) * FIELDS + field
            south_rim = ends(k, under[near_at], below[far_at])
            north_rim = ends(k, over[near_at], above[far_at])
            for level in range(HERE):
                at = field * HERE + level
                where = base + level
                if field < TRACERS:
                    target = field_ref.at[field, where]
                else:
                    target = (lon_ref, lat_ref, kab_ref)[field - TRACERS].at[where]
                target[low, main] = under[at]
                target[top, main] = over[at]
                target[low, wing] = rim(south_rim, EDGE * (HERE + level))
                target[top, wing] = rim(north_rim, EDGE * level)
    kab_ref[LEVELS - 1] = jnp.zeros((TALL, WIDE), jnp.float32)
    last_tile = TALL // 8 - 1

    def outer(i, _):
        eliminate_tile(i * last_tile, kab_ref, inv_ref, cp_ref)
        return 0

    lax.fori_loop(0, 2, outer, 0)

    def one_step(step, _):
        def solve(i, _):
            tile = jnp.where(step == 0, i * last_tile, i)
            solve_tile(tile, field_ref, solved_ref, kab_ref, inv_ref, cp_ref, red_ref)
            return 0

        lax.fori_loop(0, jnp.where(step == 0, 2, TALL // 8), solve, 0)

        def weigh(tile, _):
            at = pl.ds(pl.multiple_of(tile * 8 + EDGE, 8), 8)
            to = pl.ds(pl.multiple_of(tile * 8, 8), 8)
            for tracer in range(TRACERS):
                total = jnp.zeros((8, HALF), jnp.float32)
                for level in range(LEVELS):
                    total = total + inj_ref[tracer, level] * solved_ref[tracer, level, at, main]
                weights[step * TRACERS + tracer, to, :] = total
            return 0

        lax.fori_loop(0, ROWS // 8, weigh, 0)

        @pl.when(step < STEPS - 1)
        def _():
            advect_tiles(
                jnp.where(step == 0, TILES - 2, TILES),
                lambda i: jnp.where((step == 0) & (i >= 2), i + 2, i),
                field_ref, solved_ref, lon_ref, lat_ref,
            )

        @pl.when(step == STEPS - 1)
        def _():
            advect_tiles(ROWS // 8, lambda i: i + 1, field_ref, solved_ref, lon_ref, lat_ref, False)

        return 0

    lax.fori_loop(0, STEPS, one_step, 0)

    for tracer in range(TRACERS):
        flux = prior[tracer, :, mine].astype(jnp.float32)
        for step in range(STEPS):
            weights[step * TRACERS + tracer] = weights[step * TRACERS + tracer] * flux
        for level in range(HERE):
            kept[tracer, level] = field_ref[tracer, k * HERE + level, mid, main]
            returned[tracer, level] = field_ref[tracer, (1 - k) * HERE + level, mid, main]


def regions(side, weights, ids, sums, onehot, coarse, fine):
    mine = half_at(side[0])
    count = STEPS * TRACERS
    which = lax.broadcasted_iota(jnp.int32, (HI, HALF), 0)
    blank = jnp.zeros((SLOT - count, HALF), jnp.float32)
    nothing = jnp.zeros((SLOT, HALF), jnp.float32)
    for row in range(ROWS):
        at = slice(row * HALF, (row + 1) * HALF)
        region = ids[row : row + 1, mine]
        onehot[:, at] = jnp.where(which == region // LO, 1.0, 0.0).astype(jnp.bfloat16)
        value = jnp.concatenate([weights[:, row, :], blank], axis=0)
        big = value.astype(jnp.bfloat16).astype(jnp.float32)
        small = value - big
        for low in range(LO):
            here = region % LO == low
            to = slice(low * SLOT, (low + 1) * SLOT)
            coarse[to, at] = jnp.where(here, big, nothing).astype(jnp.bfloat16)
            fine[to, at] = jnp.where(here, small, nothing).astype(jnp.bfloat16)
    dims = (((1,), (1,)), ((), ()))
    total = lax.dot_general(onehot[...], coarse[...], dims, preferred_element_type=jnp.float32)
    total = total + lax.dot_general(onehot[...], fine[...], dims, preferred_element_type=jnp.float32)
    sums[pl.ds(0, HI, stride=2)] = total[:, :HALF]
    sums[pl.ds(1, HI, stride=2)] = total[:, HALF:]


def join(side, kept, received, out):
    k = side[0]
    for tracer in range(TRACERS):
        for level in range(HERE):
            out[tracer, level, :, half_at(k)] = kept[tracer, level]
            out[tracer, level, :, half_at(1 - k)] = received[tracer, level]


def body(adjoint, courant_lon, courant_lat, mixing, injection, prior_flux, region_ids):
    lon_count = lax.axis_size("lon")
    lat_count = lax.axis_size("lat")
    side = lax.axis_index("lev").astype(jnp.int32).reshape(1)
    raw = tuple(
        pltpu.with_memory_space_constraint(x, pltpu.HBM) for x in (adjoint, courant_lon, courant_lat, mixing)
    )
    own = tuple(hold(x) for x in (adjoint, courant_lon, courant_lat, mixing))
    injection = hold(injection)

    strip = MAIN + FIELDS
    _, edge_cross, edge_same, edge_near, to_partner, first, last = call(
        pack,
        (
            *(near(FIELDS, FOLD, HALF) for _ in range(4)),
            near(PLANES, ROWS, HALF),
            near(strip, EDGE, HALF),
            near(strip, EDGE, HALF),
        ),
        (side, injection, *raw),
        1,
    )
    same = []
    cross = []
    for i in range(lon_count):
        after = (i + 1) % lon_count
        same += [(2 * i, 2 * after), (2 * after + 1, 2 * i + 1)]
        cross += [(2 * i + 1, 2 * after), (2 * after, 2 * i + 1)]
    north = [(j, j + 1) for j in range(lat_count - 1)]
    south = [(j + 1, j) for j in range(lat_count - 1)]
    lon_cross = permute(edge_cross, ("lon", "lev"), cross)
    lon_same = permute(edge_same, ("lon", "lev"), same)

    partner = permute(to_partner, "lev", [(0, 1), (1, 0)])
    own_below = permute(last, "lat", north)
    own_above = permute(first, "lat", south)

    strip = MAIN + 3 * FIELDS
    first, last = call(
        strips,
        (near(strip, EDGE, HALF), near(strip, EDGE, HALF)),
        (partner, lon_same, lon_cross, own_below, own_above),
        0,
    )
    below = permute(last, "lat", north)
    above = permute(first, "lat", south)

    block = (LEVELS, TALL, WIDE)
    tile = pltpu.VMEM((TRACERS, LEVELS, 8, WIDE), jnp.float32)
    arrays = (near(TRACERS, *block), near(TRACERS, *block), *(near(*block) for _ in range(5)))
    *state, inj = call(
        prepare,
        (*arrays, near(TRACERS, LEVELS, 8, HALF)),
        (side, injection, *own, partner, edge_near, lon_same, lon_cross),
        1,
        [tile],
    )
    kept, returned, weights = call(
        steps,
        (
            near(TRACERS, HERE, ROWS, HALF),
            near(TRACERS, HERE, ROWS, HALF),
            near(STEPS * TRACERS, ROWS, HALF),
            *arrays,
        ),
        (side, own_below, own_above, below, above, hold(prior_flux), hold(inj), *(hold(x) for x in state)),
        1,
        [tile],
        8,
        {7 + i: 3 + i for i in range(7)},
    )[:3]
    received = permute(returned, "lev", [(0, 1), (1, 0)])
    sums = call(
        regions,
        near(2 * HI, HALF),
        (side, weights, region_ids),
        1,
        [pltpu.VMEM((HI, ROWS * HALF), jnp.bfloat16) for _ in range(3)],
        12,
    )
    pieces = lax.all_to_all(sums, ("lon", "lat", "lev"), 0, 0, tiled=True)
    region_grad = jnp.sum(pieces, axis=0).reshape(-1, SLOT)[:, : STEPS * TRACERS]
    adjoint_out = call(join, f32(*adjoint.shape), (side, kept, received), 1)
    return (adjoint_out, region_grad)


def solution(mesh):
    placed = (
        P(None, "lev", "lat", "lon"),
        P("lev", "lat", "lon"),
        P("lev", "lat", "lon"),
        P("lev", "lat", "lon"),
        P(None, "lev"),
        P(None, "lat", "lon"),
        P("lat", "lon"),
    )
    return jax.shard_map(
        body,
        mesh=mesh,
        in_specs=placed,
        out_specs=(P(None, "lev", "lat", "lon"), P(("lon", "lat", "lev"), None)),
        check_vma=False,
    )
```

```python
import jax
import jax.numpy as jnp
from jax import lax
from jax.experimental import pallas as pl
from jax.experimental.pallas import tpu as pltpu
from jax.sharding import PartitionSpec as P

STEPS = 6
TRACERS = 4
FIELDS = TRACERS + 3
HERE = 8
LEVELS = 16
ROWS = 32
HALF = 128
EDGE = 8
TALL = ROWS + 2 * EDGE
WIDE = 2 * HALF
MAIN = FIELDS * HERE
FOLD = 2 * EDGE
PLANES = MAIN + (FIELDS + 1) // 2 + 1
HI = 256
LO = 8
SLOT = 32

VMEM = pl.BlockSpec(memory_space=pltpu.VMEM)
SMEM = pl.BlockSpec(memory_space=pltpu.SMEM)
MIB = 1024 * 1024


def call(kernel, out_shape, operands, scalars, scratch=(), limit=8, alias=None):
    specs = [SMEM] * scalars + [VMEM] * (len(operands) - scalars)
    many = isinstance(out_shape, (tuple, list))
    return pl.pallas_call(
        kernel,
        out_shape=out_shape,
        in_specs=specs,
        out_specs=tuple(VMEM for _ in out_shape) if many else VMEM,
        scratch_shapes=list(scratch),
        compiler_params=pltpu.CompilerParams(vmem_limit_bytes=limit * MIB),
        name=kernel.__name__,
        input_output_aliases=alias or {},
    )(*operands)


def f32(*shape):
    return jax.ShapeDtypeStruct(shape, jnp.float32)


def near(*shape):
    return pltpu.VMEM(shape, jnp.float32)


def hold(x):
    return pltpu.with_memory_space_constraint(x, pltpu.VMEM)


def permute(x, axes, pairs):
    return hold(lax.ppermute(x, axes, pairs))


def half_at(which):
    return pl.ds(pl.multiple_of(which * HALF, HALF), HALF)


def own_plane(refs, field, level, rows, lanes):
    adjoint, lon_wind, lat_wind, mixing = refs
    if field < TRACERS:
        return adjoint[field, level, rows, lanes]
    ref = (lon_wind, lat_wind, mixing)[field - TRACERS]
    return ref[level, rows, lanes].astype(jnp.float32)


def pack_edges(side, adjoint, lon_wind, lat_wind, mixing, inner, cross, same, near):
    refs = (adjoint, lon_wind, lat_wind, mixing)
    k = side[0]
    mine = half_at(k)
    other = half_at(1 - k)
    slot = lax.broadcasted_iota(jnp.int32, (FOLD, HALF), 1) // EDGE
    upper = slice(0, FOLD)
    lower = slice(FOLD, ROWS)
    west = k == 0

    def packed(planes, begin):
        out = jnp.zeros((FOLD, HALF), jnp.float32)
        for level, plane in enumerate(planes):
            for rows, to in ((upper, level), (lower, HERE + level)):
                shift = (EDGE * to - begin) % HALF
                moved = pltpu.roll(plane[rows], shift, 1) if shift else plane[rows]
                out = jnp.where(slot == to, moved, out)
        return out

    for field in range(FIELDS):
        planes = [own_plane(refs, field, level, slice(0, ROWS), mine) for level in range(HERE)]
        low = packed(planes, 0)
        high = packed(planes, HALF - EDGE)
        inner[field] = jnp.where(west, high, low)
        cross[field] = jnp.where(west, low, high)
        planes = [own_plane(refs, field, level, slice(0, ROWS), other) for level in range(HERE)]
        low = packed(planes, 0)
        high = packed(planes, HALF - EDGE)
        same[field] = jnp.where(west, high, low)
        near[field] = jnp.where(west, low, high)


def pack_main(side, injection, adjoint, lon_wind, lat_wind, mixing, inner, near, to_partner, first, last):
    refs = (adjoint, lon_wind, lat_wind, mixing)
    mine = half_at(side[0])
    other = half_at(1 - side[0])
    for field in range(FIELDS):
        for level in range(HERE):
            at = field * HERE + level
            to_partner[at] = own_plane(refs, field, level, slice(0, ROWS), other)
            plane = own_plane(refs, field, level, slice(0, ROWS), mine)
            first[at] = plane[:EDGE]
            last[at] = plane[ROWS - EDGE :]
        to_partner[MAIN + field // 2, pl.ds(field % 2 * FOLD, FOLD), :] = inner[field]
        first[MAIN + field] = near[field, :EDGE]
        last[MAIN + field] = near[field, EDGE:]
    for tracer in range(TRACERS):
        for level in range(HERE):
            row = tracer * HERE + level
            to_partner[PLANES - 1, row : row + 1, :] = jnp.broadcast_to(
                injection[tracer : tracer + 1, level : level + 1], (1, HALF)
            )


def pack(
    side, injection, adjoint, lon_wind, lat_wind, mixing, inner, cross, same, near, to_partner, first, last
):
    pack_edges(side, adjoint, lon_wind, lat_wind, mixing, inner, cross, same, near)
    pack_main(side, injection, adjoint, lon_wind, lat_wind, mixing, inner, near, to_partner, first, last)


def strips(partner, lon_same, lon_cross, own_below, own_above, first, last):
    first[0:MAIN] = partner[0:MAIN, 0:EDGE, :]
    last[0:MAIN] = partner[0:MAIN, ROWS - EDGE : ROWS, :]
    for field in range(FIELDS):
        begin = field % 2 * FOLD
        first[MAIN + field] = partner[MAIN + field // 2, begin : begin + EDGE, :]
        last[MAIN + field] = partner[MAIN + field // 2, begin + EDGE : begin + FOLD, :]
    for group, rims in enumerate((lon_same, lon_cross)):
        at = slice(MAIN + (1 + group) * FIELDS, MAIN + (2 + group) * FIELDS)
        first[at] = rims[:, :EDGE, :]
        last[at] = rims[:, EDGE:, :]


def turned(x, shift):
    return pltpu.roll(x, shift % HALF, 1) if shift % HALF else x


def rim(pair, begin):
    ahead, behind = pair
    lane = lax.broadcasted_iota(jnp.int32, ahead.shape, 1) < HALF // 2
    return jnp.where(lane, turned(ahead, -begin), turned(behind, -begin - EDGE))


def ends(k, inside, outside):
    return jnp.where(k == 0, inside, outside), jnp.where(k == 0, outside, inside)


MAIN_LANES = slice(0, HALF)
WING_LANES = slice(HALF, WIDE)


def eliminate_tile(tile, kab_ref, inv_ref, cp_ref):
    at = pl.ds(pl.multiple_of(tile * 8, 8), 8)
    carried = jnp.zeros((8, WIDE), jnp.float32)
    kbelow = jnp.zeros((8, WIDE), jnp.float32)
    for level in range(LEVELS):
        kabove = kab_ref[level, at, :]
        inverse = 1.0 / (1.0 + kabove + kbelow * (1.0 + carried))
        carried = -kabove * inverse
        inv_ref[level, at, :] = inverse
        cp_ref[level, at, :] = carried
        kbelow = kabove


def solve_tile(tile, field_ref, solved_ref, kab_ref, inv_ref, cp_ref, red_ref):
    at = pl.ds(pl.multiple_of(tile * 8, 8), 8)
    carried = [None] * TRACERS
    for level in range(LEVELS):
        inverse = inv_ref[level, at, :]
        if level:
            kbelow = kab_ref[level - 1, at, :]
        for tracer in range(TRACERS):
            rhs = field_ref[tracer, level, at, :]
            if level:
                rhs = rhs + kbelow * carried[tracer]
            carried[tracer] = rhs * inverse
            red_ref[tracer, level] = carried[tracer]
    for tracer in range(TRACERS):
        solved_ref[tracer, LEVELS - 1, at, :] = carried[tracer]
    for level in reversed(range(LEVELS - 1)):
        cprime = cp_ref[level, at, :]
        for tracer in range(TRACERS):
            carried[tracer] = red_ref[tracer, level] - cprime * carried[tracer]
            solved_ref[tracer, level, at, :] = carried[tracer]


TILES = TALL // 8


def rows_of(tile):
    return slice(tile % TILES * 8, tile % TILES * 8 + 8)


def advect_tiles(tiles, field_ref, solved_ref, lon_ref, lat_ref, wings=True):
    sides = (MAIN_LANES, WING_LANES)
    count = 2 if wings else 1
    row = lax.broadcasted_iota(jnp.int32, (8, HALF), 0)
    lane = lax.broadcasted_iota(jnp.int32, (8, HALF), 1)

    def one_level(level, _):
        for tile in tiles:
            at = rows_of(tile)
            rates = []
            for side in sides[:count]:
                lon = lon_ref[level, at, side]
                lat = lat_ref[level, at, side]
                rates.append((lon > 0.0, lat > 0.0, jnp.abs(lon), jnp.abs(lat)))
            for tracer in range(TRACERS):
                cells = [solved_ref[tracer, level, at, side] for side in sides]
                ahead = [pltpu.roll(c, HALF - 1, 1) for c in cells]
                behind = [pltpu.roll(c, 1, 1) for c in cells]
                for i, side in enumerate(sides[:count]):
                    east, north, lon, lat = rates[i]
                    here = cells[i]
                    along = jnp.where(
                        east,
                        jnp.where(lane == HALF - 1, ahead[1 - i], ahead[i]),
                        jnp.where(lane == 0, behind[1 - i], behind[i]),
                    )
                    after = solved_ref[tracer, level, rows_of(tile + 1), side]
                    before = solved_ref[tracer, level, rows_of(tile - 1), side]
                    across = jnp.where(
                        north,
                        jnp.where(row == 7, pltpu.roll(after, 7, 0), pltpu.roll(here, 7, 0)),
                        jnp.where(row == 0, pltpu.roll(before, 1, 0), pltpu.roll(here, 1, 0)),
                    )
                    field_ref[tracer, level, at, side] = here + lon * (along - here) + lat * (across - here)
        return 0

    lax.fori_loop(0, LEVELS, one_level, 0)


def prepare(
    side, injection, adjoint, lon_wind, lat_wind, mixing, partner, near, lon_same, lon_cross,
    field_ref, solved_ref, lon_ref, lat_ref, kab_ref, inv_ref, cp_ref, inj_ref, red_ref,
):
    refs = (adjoint, lon_wind, lat_wind, mixing)
    k = side[0]
    mine = half_at(k)
    for group in range(2):
        base = (k if group == 0 else 1 - k) * HERE
        for field in range(FIELDS):
            begin = field % 2 * FOLD
            inside = near[field] if group == 0 else partner[MAIN + field // 2, begin : begin + FOLD, :]
            pair = ends(k, inside, (lon_same, lon_cross)[group][field])
            for level in range(HERE):
                where = base + level
                if field < TRACERS:
                    target = field_ref.at[field, where]
                else:
                    target = (lon_ref, lat_ref, kab_ref)[field - TRACERS].at[where]
                if group == 0:
                    plane = own_plane(refs, field, level, slice(0, ROWS), mine)
                else:
                    plane = partner[field * HERE + level]
                target[EDGE : EDGE + ROWS, MAIN_LANES] = plane
                target[EDGE : EDGE + FOLD, WING_LANES] = rim(pair, EDGE * level)
                target[EDGE + FOLD : EDGE + ROWS, WING_LANES] = rim(pair, EDGE * (HERE + level))
    for tracer in range(TRACERS):
        for level in range(HERE):
            row = tracer * HERE + level
            inj_ref[tracer, pl.ds(k * HERE + level, 1)] = jnp.broadcast_to(
                injection[tracer : tracer + 1, level : level + 1][None], (1, 8, HALF)
            )
            inj_ref[tracer, pl.ds((1 - k) * HERE + level, 1)] = jnp.broadcast_to(
                partner[PLANES - 1, row : row + 1, :][None], (1, 8, HALF)
            )
    kab_ref[LEVELS - 1] = jnp.zeros((TALL, WIDE), jnp.float32)

    def inner(tile, _):
        eliminate_tile(tile, kab_ref, inv_ref, cp_ref)
        solve_tile(tile, field_ref, solved_ref, kab_ref, inv_ref, cp_ref, red_ref)
        return 0

    lax.fori_loop(1, 1 + ROWS // 8, inner, 0)
    advect_tiles((2, 3), field_ref, solved_ref, lon_ref, lat_ref)


def steps(
    side, own_below, own_above, below, above, prior, inj_ref,
    field_in, solved_in, lon_in, lat_in, kab_in, inv_in, cp_in,
    kept, returned, weights,
    field_ref, solved_ref, lon_ref, lat_ref, kab_ref, inv_ref, cp_ref, red_ref,
):
    k = side[0]
    mine = half_at(k)
    mid = slice(EDGE, EDGE + ROWS)
    low = slice(0, EDGE)
    top = slice(EDGE + ROWS, TALL)
    main = MAIN_LANES
    wing = WING_LANES
    for group in range(2):
        base = (k if group == 0 else 1 - k) * HERE
        under, over = (own_below, own_above) if group == 0 else (below, above)
        for field in range(FIELDS):
            near_at = MAIN + field
            far_at = MAIN + (1 + group) * FIELDS + field
            south_rim = ends(k, under[near_at], below[far_at])
            north_rim = ends(k, over[near_at], above[far_at])
            for level in range(HERE):
                at = field * HERE + level
                where = base + level
                if field < TRACERS:
                    target = field_ref.at[field, where]
                else:
                    target = (lon_ref, lat_ref, kab_ref)[field - TRACERS].at[where]
                target[low, main] = under[at]
                target[top, main] = over[at]
                target[low, wing] = rim(south_rim, EDGE * (HERE + level))
                target[top, wing] = rim(north_rim, EDGE * level)
    kab_ref[LEVELS - 1] = jnp.zeros((TALL, WIDE), jnp.float32)
    last_tile = TALL // 8 - 1

    def outer(i, _):
        eliminate_tile(i * last_tile, kab_ref, inv_ref, cp_ref)
        return 0

    lax.fori_loop(0, 2, outer, 0)

    def one_step(step, _):
        def solve(i, _):
            tile = jnp.where(step == 0, i * last_tile, i)
            solve_tile(tile, field_ref, solved_ref, kab_ref, inv_ref, cp_ref, red_ref)
            return 0

        lax.fori_loop(0, jnp.where(step == 0, 2, TALL // 8), solve, 0)

        def weigh(tile, _):
            at = pl.ds(pl.multiple_of(tile * 8 + EDGE, 8), 8)
            to = pl.ds(pl.multiple_of(tile * 8, 8), 8)
            for tracer in range(TRACERS):
                total = jnp.zeros((8, HALF), jnp.float32)
                for level in range(LEVELS):
                    total = total + inj_ref[tracer, level] * solved_ref[tracer, level, at, main]
                weights[step * TRACERS + tracer, to, :] = total
            return 0

        lax.fori_loop(0, ROWS // 8, weigh, 0)

        buffers = (field_ref, solved_ref, lon_ref, lat_ref)

        @pl.when(step == 0)
        def _():
            advect_tiles((0, 1, 4, 5), *buffers)

        @pl.when((step > 0) & (step < STEPS - 1))
        def _():
            advect_tiles(range(TILES), *buffers)

        @pl.when(step == STEPS - 1)
        def _():
            advect_tiles(range(1, 1 + ROWS // 8), *buffers, wings=False)

        return 0

    lax.fori_loop(0, STEPS, one_step, 0)

    for tracer in range(TRACERS):
        flux = prior[tracer, :, mine].astype(jnp.float32)
        for step in range(STEPS):
            weights[step * TRACERS + tracer] = weights[step * TRACERS + tracer] * flux
        for level in range(HERE):
            kept[tracer, level] = field_ref[tracer, k * HERE + level, mid, main]
            returned[tracer, level] = field_ref[tracer, (1 - k) * HERE + level, mid, main]


def regions(side, weights, ids, sums, onehot, coarse, fine):
    mine = half_at(side[0])
    count = STEPS * TRACERS
    which = lax.broadcasted_iota(jnp.int32, (HI, HALF), 0)
    blank = jnp.zeros((SLOT - count, HALF), jnp.float32)
    nothing = jnp.zeros((SLOT, HALF), jnp.float32)
    for row in range(ROWS):
        at = slice(row * HALF, (row + 1) * HALF)
        region = ids[row : row + 1, mine]
        onehot[:, at] = jnp.where(which == region // LO, 1.0, 0.0).astype(jnp.bfloat16)
        value = jnp.concatenate([weights[:, row, :], blank], axis=0)
        big = value.astype(jnp.bfloat16).astype(jnp.float32)
        small = value - big
        for low in range(LO):
            here = region % LO == low
            to = slice(low * SLOT, (low + 1) * SLOT)
            coarse[to, at] = jnp.where(here, big, nothing).astype(jnp.bfloat16)
            fine[to, at] = jnp.where(here, small, nothing).astype(jnp.bfloat16)
    dims = (((1,), (1,)), ((), ()))
    total = lax.dot_general(onehot[...], coarse[...], dims, preferred_element_type=jnp.float32)
    total = total + lax.dot_general(onehot[...], fine[...], dims, preferred_element_type=jnp.float32)
    sums[pl.ds(0, HI, stride=2)] = total[:, :HALF]
    sums[pl.ds(1, HI, stride=2)] = total[:, HALF:]


def join(side, kept, received, out):
    k = side[0]
    for tracer in range(TRACERS):
        for level in range(HERE):
            out[tracer, level, :, half_at(k)] = kept[tracer, level]
            out[tracer, level, :, half_at(1 - k)] = received[tracer, level]


def body(adjoint, courant_lon, courant_lat, mixing, injection, prior_flux, region_ids):
    lon_count = lax.axis_size("lon")
    lat_count = lax.axis_size("lat")
    side = lax.axis_index("lev").astype(jnp.int32).reshape(1)
    raw = tuple(
        pltpu.with_memory_space_constraint(x, pltpu.HBM) for x in (adjoint, courant_lon, courant_lat, mixing)
    )
    own = tuple(hold(x) for x in (adjoint, courant_lon, courant_lat, mixing))
    injection = hold(injection)

    strip = MAIN + FIELDS
    _, edge_cross, edge_same, edge_near, to_partner, first, last = call(
        pack,
        (
            *(near(FIELDS, FOLD, HALF) for _ in range(4)),
            near(PLANES, ROWS, HALF),
            near(strip, EDGE, HALF),
            near(strip, EDGE, HALF),
        ),
        (side, injection, *raw),
        1,
    )
    same = []
    cross = []
    for i in range(lon_count):
        after = (i + 1) % lon_count
        same += [(2 * i, 2 * after), (2 * after + 1, 2 * i + 1)]
        cross += [(2 * i + 1, 2 * after), (2 * after, 2 * i + 1)]
    north = [(j, j + 1) for j in range(lat_count - 1)]
    south = [(j + 1, j) for j in range(lat_count - 1)]
    lon_cross = permute(edge_cross, ("lon", "lev"), cross)
    lon_same = permute(edge_same, ("lon", "lev"), same)

    partner = permute(to_partner, "lev", [(0, 1), (1, 0)])
    own_below = permute(last, "lat", north)
    own_above = permute(first, "lat", south)

    strip = MAIN + 3 * FIELDS
    first, last = call(
        strips,
        (near(strip, EDGE, HALF), near(strip, EDGE, HALF)),
        (partner, lon_same, lon_cross, own_below, own_above),
        0,
    )
    below = permute(last, "lat", north)
    above = permute(first, "lat", south)

    block = (LEVELS, TALL, WIDE)
    tile = pltpu.VMEM((TRACERS, LEVELS, 8, WIDE), jnp.float32)
    arrays = (near(TRACERS, *block), near(TRACERS, *block), *(near(*block) for _ in range(5)))
    *state, inj = call(
        prepare,
        (*arrays, near(TRACERS, LEVELS, 8, HALF)),
        (side, injection, *own, partner, edge_near, lon_same, lon_cross),
        1,
        [tile],
    )
    kept, returned, weights = call(
        steps,
        (
            near(TRACERS, HERE, ROWS, HALF),
            near(TRACERS, HERE, ROWS, HALF),
            near(STEPS * TRACERS, ROWS, HALF),
            *arrays,
        ),
        (side, own_below, own_above, below, above, hold(prior_flux), hold(inj), *(hold(x) for x in state)),
        1,
        [tile],
        8,
        {7 + i: 3 + i for i in range(7)},
    )[:3]
    received = permute(returned, "lev", [(0, 1), (1, 0)])
    sums = call(
        regions,
        near(2 * HI, HALF),
        (side, weights, region_ids),
        1,
        [pltpu.VMEM((HI, ROWS * HALF), jnp.bfloat16) for _ in range(3)],
        12,
    )
    pieces = lax.all_to_all(sums, ("lon", "lat", "lev"), 0, 0, tiled=True)
    region_grad = jnp.sum(pieces, axis=0).reshape(-1, SLOT)[:, : STEPS * TRACERS]
    adjoint_out = call(join, f32(*adjoint.shape), (side, kept, received), 1)
    return (adjoint_out, region_grad)


def solution(mesh):
    placed = (
        P(None, "lev", "lat", "lon"),
        P("lev", "lat", "lon"),
        P("lev", "lat", "lon"),
        P("lev", "lat", "lon"),
        P(None, "lev"),
        P(None, "lat", "lon"),
        P("lat", "lon"),
    )
    return jax.shard_map(
        body,
        mesh=mesh,
        in_specs=placed,
        out_specs=(P(None, "lev", "lat", "lon"), P(("lon", "lat", "lev"), None)),
        check_vma=False,
    )
```

```python
import jax
import jax.numpy as jnp
from jax import lax
from jax.experimental import pallas as pl
from jax.experimental.pallas import tpu as pltpu
from jax.sharding import PartitionSpec as P

STEPS = 6
TRACERS = 4
FIELDS = TRACERS + 3
HERE = 8
LEVELS = 16
ROWS = 32
HALF = 128
EDGE = 8
TALL = ROWS + 2 * EDGE
WIDE = 2 * HALF
MAIN = FIELDS * HERE
FOLD = 2 * EDGE
PLANES = MAIN + (FIELDS + 1) // 2 + 1
HI = 256
LO = 8
SLOT = 32

VMEM = pl.BlockSpec(memory_space=pltpu.VMEM)
SMEM = pl.BlockSpec(memory_space=pltpu.SMEM)
MIB = 1024 * 1024


def call(kernel, out_shape, operands, scalars, scratch=(), limit=8, alias=None):
    specs = [SMEM] * scalars + [VMEM] * (len(operands) - scalars)
    many = isinstance(out_shape, (tuple, list))
    return pl.pallas_call(
        kernel,
        out_shape=out_shape,
        in_specs=specs,
        out_specs=tuple(VMEM for _ in out_shape) if many else VMEM,
        scratch_shapes=list(scratch),
        compiler_params=pltpu.CompilerParams(vmem_limit_bytes=limit * MIB),
        name=kernel.__name__,
        input_output_aliases=alias or {},
    )(*operands)


def f32(*shape):
    return jax.ShapeDtypeStruct(shape, jnp.float32)


def near(*shape):
    return pltpu.VMEM(shape, jnp.float32)


def hold(x):
    return pltpu.with_memory_space_constraint(x, pltpu.VMEM)


def permute(x, axes, pairs):
    return hold(lax.ppermute(x, axes, pairs))


def half_at(which):
    return pl.ds(pl.multiple_of(which * HALF, HALF), HALF)


def own_plane(refs, field, level, rows, lanes):
    adjoint, lon_wind, lat_wind, mixing = refs
    if field < TRACERS:
        return adjoint[field, level, rows, lanes]
    ref = (lon_wind, lat_wind, mixing)[field - TRACERS]
    return ref[level, rows, lanes].astype(jnp.float32)


def pack_edges(side, adjoint, lon_wind, lat_wind, mixing, inner, cross, same, near):
    refs = (adjoint, lon_wind, lat_wind, mixing)
    k = side[0]
    mine = half_at(k)
    other = half_at(1 - k)
    slot = lax.broadcasted_iota(jnp.int32, (FOLD, HALF), 1) // EDGE
    upper = slice(0, FOLD)
    lower = slice(FOLD, ROWS)
    west = k == 0

    def packed(planes, begin):
        out = jnp.zeros((FOLD, HALF), jnp.float32)
        for level, plane in enumerate(planes):
            for rows, to in ((upper, level), (lower, HERE + level)):
                shift = (EDGE * to - begin) % HALF
                moved = pltpu.roll(plane[rows], shift, 1) if shift else plane[rows]
                out = jnp.where(slot == to, moved, out)
        return out

    for field in range(FIELDS):
        planes = [own_plane(refs, field, level, slice(0, ROWS), mine) for level in range(HERE)]
        low = packed(planes, 0)
        high = packed(planes, HALF - EDGE)
        inner[field] = jnp.where(west, high, low)
        cross[field] = jnp.where(west, low, high)
        planes = [own_plane(refs, field, level, slice(0, ROWS), other) for level in range(HERE)]
        low = packed(planes, 0)
        high = packed(planes, HALF - EDGE)
        same[field] = jnp.where(west, high, low)
        near[field] = jnp.where(west, low, high)


def pack_main(side, injection, adjoint, lon_wind, lat_wind, mixing, inner, near, to_partner, first, last):
    refs = (adjoint, lon_wind, lat_wind, mixing)
    mine = half_at(side[0])
    other = half_at(1 - side[0])
    for field in range(FIELDS):
        for level in range(HERE):
            at = field * HERE + level
            to_partner[at] = own_plane(refs, field, level, slice(0, ROWS), other)
            plane = own_plane(refs, field, level, slice(0, ROWS), mine)
            first[at] = plane[:EDGE]
            last[at] = plane[ROWS - EDGE :]
        to_partner[MAIN + field // 2, pl.ds(field % 2 * FOLD, FOLD), :] = inner[field]
        first[MAIN + field] = near[field, :EDGE]
        last[MAIN + field] = near[field, EDGE:]
    for tracer in range(TRACERS):
        for level in range(HERE):
            row = tracer * HERE + level
            to_partner[PLANES - 1, row : row + 1, :] = jnp.broadcast_to(
                injection[tracer : tracer + 1, level : level + 1], (1, HALF)
            )


def pack(
    side, injection, adjoint, lon_wind, lat_wind, mixing, inner, cross, same, near, to_partner, first, last
):
    pack_edges(side, adjoint, lon_wind, lat_wind, mixing, inner, cross, same, near)
    pack_main(side, injection, adjoint, lon_wind, lat_wind, mixing, inner, near, to_partner, first, last)


def strips(partner, lon_same, lon_cross, own_below, own_above, first, last):
    first[0:MAIN] = partner[0:MAIN, 0:EDGE, :]
    last[0:MAIN] = partner[0:MAIN, ROWS - EDGE : ROWS, :]
    for field in range(FIELDS):
        begin = field % 2 * FOLD
        first[MAIN + field] = partner[MAIN + field // 2, begin : begin + EDGE, :]
        last[MAIN + field] = partner[MAIN + field // 2, begin + EDGE : begin + FOLD, :]
    for group, rims in enumerate((lon_same, lon_cross)):
        at = slice(MAIN + (1 + group) * FIELDS, MAIN + (2 + group) * FIELDS)
        first[at] = rims[:, :EDGE, :]
        last[at] = rims[:, EDGE:, :]


def turned(x, shift):
    return pltpu.roll(x, shift % HALF, 1) if shift % HALF else x


def rim(pair, begin):
    ahead, behind = pair
    lane = lax.broadcasted_iota(jnp.int32, ahead.shape, 1) < HALF // 2
    return jnp.where(lane, turned(ahead, -begin), turned(behind, -begin - EDGE))


def ends(k, inside, outside):
    return jnp.where(k == 0, inside, outside), jnp.where(k == 0, outside, inside)


MAIN_LANES = slice(0, HALF)
WING_LANES = slice(HALF, WIDE)


def eliminate_tile(tile, kab_ref, inv_ref, cp_ref):
    at = pl.ds(pl.multiple_of(tile * 8, 8), 8)
    carried = jnp.zeros((8, WIDE), jnp.float32)
    kbelow = jnp.zeros((8, WIDE), jnp.float32)
    for level in range(LEVELS):
        kabove = kab_ref[level, at, :]
        inverse = 1.0 / (1.0 + kabove + kbelow * (1.0 + carried))
        carried = -kabove * inverse
        inv_ref[level, at, :] = inverse
        cp_ref[level, at, :] = carried
        kbelow = kabove


def solve_tile(tile, field_ref, solved_ref, kab_ref, inv_ref, cp_ref, red_ref):
    at = pl.ds(pl.multiple_of(tile * 8, 8), 8)
    carried = [None] * TRACERS
    for level in range(LEVELS):
        inverse = inv_ref[level, at, :]
        if level:
            kbelow = kab_ref[level - 1, at, :]
        for tracer in range(TRACERS):
            rhs = field_ref[tracer, level, at, :]
            if level:
                rhs = rhs + kbelow * carried[tracer]
            carried[tracer] = rhs * inverse
            red_ref[tracer, level] = carried[tracer]
    for tracer in range(TRACERS):
        solved_ref[tracer, LEVELS - 1, at, :] = carried[tracer]
    for level in reversed(range(LEVELS - 1)):
        cprime = cp_ref[level, at, :]
        for tracer in range(TRACERS):
            carried[tracer] = red_ref[tracer, level] - cprime * carried[tracer]
            solved_ref[tracer, level, at, :] = carried[tracer]


TILES = TALL // 8


def rows_of(tile):
    return slice(tile % TILES * 8, tile % TILES * 8 + 8)


def advect_tiles(tiles, field_ref, solved_ref, lon_ref, lat_ref, wings=True):
    sides = (MAIN_LANES, WING_LANES)
    count = 2 if wings else 1
    row = lax.broadcasted_iota(jnp.int32, (8, HALF), 0)
    lane = lax.broadcasted_iota(jnp.int32, (8, HALF), 1)

    def one_level(level, _):
        for tile in tiles:
            at = rows_of(tile)
            rates = []
            for side in sides[:count]:
                lon = lon_ref[level, at, side]
                lat = lat_ref[level, at, side]
                rates.append((lon > 0.0, lat > 0.0, jnp.abs(lon), jnp.abs(lat)))
            for tracer in range(TRACERS):
                cells = [solved_ref[tracer, level, at, side] for side in sides]
                ahead = [pltpu.roll(c, HALF - 1, 1) for c in cells]
                behind = [pltpu.roll(c, 1, 1) for c in cells]
                for i, side in enumerate(sides[:count]):
                    east, north, lon, lat = rates[i]
                    here = cells[i]
                    along = jnp.where(
                        east,
                        jnp.where(lane == HALF - 1, ahead[1 - i], ahead[i]),
                        jnp.where(lane == 0, behind[1 - i], behind[i]),
                    )
                    after = solved_ref[tracer, level, rows_of(tile + 1), side]
                    before = solved_ref[tracer, level, rows_of(tile - 1), side]
                    across = jnp.where(
                        north,
                        jnp.where(row == 7, pltpu.roll(after, 7, 0), pltpu.roll(here, 7, 0)),
                        jnp.where(row == 0, pltpu.roll(before, 1, 0), pltpu.roll(here, 1, 0)),
                    )
                    field_ref[tracer, level, at, side] = here + lon * (along - here) + lat * (across - here)
        return 0

    lax.fori_loop(0, LEVELS, one_level, 0)


def prepare(
    side, injection, adjoint, lon_wind, lat_wind, mixing, partner, near, lon_same, lon_cross,
    field_ref, solved_ref, lon_ref, lat_ref, kab_ref, inv_ref, cp_ref, inj_ref, red_ref,
):
    refs = (adjoint, lon_wind, lat_wind, mixing)
    k = side[0]
    mine = half_at(k)
    for group in range(2):
        base = (k if group == 0 else 1 - k) * HERE
        for field in range(FIELDS):
            begin = field % 2 * FOLD
            inside = near[field] if group == 0 else partner[MAIN + field // 2, begin : begin + FOLD, :]
            pair = ends(k, inside, (lon_same, lon_cross)[group][field])
            for level in range(HERE):
                where = base + level
                if field < TRACERS:
                    target = field_ref.at[field, where]
                else:
                    target = (lon_ref, lat_ref, kab_ref)[field - TRACERS].at[where]
                if group == 0:
                    plane = own_plane(refs, field, level, slice(0, ROWS), mine)
                else:
                    plane = partner[field * HERE + level]
                target[EDGE : EDGE + ROWS, MAIN_LANES] = plane
                target[EDGE : EDGE + FOLD, WING_LANES] = rim(pair, EDGE * level)
                target[EDGE + FOLD : EDGE + ROWS, WING_LANES] = rim(pair, EDGE * (HERE + level))
    for tracer in range(TRACERS):
        for level in range(HERE):
            row = tracer * HERE + level
            inj_ref[tracer, pl.ds(k * HERE + level, 1)] = jnp.broadcast_to(
                injection[tracer : tracer + 1, level : level + 1][None], (1, 8, HALF)
            )
            inj_ref[tracer, pl.ds((1 - k) * HERE + level, 1)] = jnp.broadcast_to(
                partner[PLANES - 1, row : row + 1, :][None], (1, 8, HALF)
            )
    kab_ref[LEVELS - 1] = jnp.zeros((TALL, WIDE), jnp.float32)

    def inner(tile, _):
        eliminate_tile(tile, kab_ref, inv_ref, cp_ref)
        solve_tile(tile, field_ref, solved_ref, kab_ref, inv_ref, cp_ref, red_ref)
        return 0

    lax.fori_loop(1, 1 + ROWS // 8, inner, 0)
    advect_tiles((2, 3), field_ref, solved_ref, lon_ref, lat_ref)


def steps(
    side, own_below, own_above, below, above, prior, inj_ref,
    field_in, solved_in, lon_in, lat_in, kab_in, inv_in, cp_in,
    kept, returned, weights,
    field_ref, solved_ref, lon_ref, lat_ref, kab_ref, inv_ref, cp_ref, red_ref,
):
    k = side[0]
    mine = half_at(k)
    mid = slice(EDGE, EDGE + ROWS)
    low = slice(0, EDGE)
    top = slice(EDGE + ROWS, TALL)
    main = MAIN_LANES
    wing = WING_LANES
    for group in range(2):
        base = (k if group == 0 else 1 - k) * HERE
        under, over = (own_below, own_above) if group == 0 else (below, above)
        for field in range(FIELDS):
            near_at = MAIN + field
            far_at = MAIN + (1 + group) * FIELDS + field
            south_rim = ends(k, under[near_at], below[far_at])
            north_rim = ends(k, over[near_at], above[far_at])
            for level in range(HERE):
                at = field * HERE + level
                where = base + level
                if field < TRACERS:
                    target = field_ref.at[field, where]
                else:
                    target = (lon_ref, lat_ref, kab_ref)[field - TRACERS].at[where]
                target[low, main] = under[at]
                target[top, main] = over[at]
                target[low, wing] = rim(south_rim, EDGE * (HERE + level))
                target[top, wing] = rim(north_rim, EDGE * level)
    kab_ref[LEVELS - 1] = jnp.zeros((TALL, WIDE), jnp.float32)
    last_tile = TALL // 8 - 1

    def outer(i, _):
        eliminate_tile(i * last_tile, kab_ref, inv_ref, cp_ref)
        return 0

    lax.fori_loop(0, 2, outer, 0)

    def one_step(step, _):
        def solve(i, _):
            tile = jnp.where(step == 0, i * last_tile, i)
            solve_tile(tile, field_ref, solved_ref, kab_ref, inv_ref, cp_ref, red_ref)
            return 0

        lax.fori_loop(0, jnp.where(step == 0, 2, TALL // 8), solve, 0)

        def weigh(tile, _):
            at = pl.ds(pl.multiple_of(tile * 8 + EDGE, 8), 8)
            to = pl.ds(pl.multiple_of(tile * 8, 8), 8)
            for tracer in range(TRACERS):
                total = jnp.zeros((8, HALF), jnp.float32)
                for level in range(LEVELS):
                    total = total + inj_ref[tracer, level] * solved_ref[tracer, level, at, main]
                weights[step * TRACERS + tracer, to, :] = total
            return 0

        lax.fori_loop(0, ROWS // 8, weigh, 0)

        buffers = (field_ref, solved_ref, lon_ref, lat_ref)

        @pl.when(step == 0)
        def _():
            advect_tiles((0, 1, 4, 5), *buffers)

        @pl.when((step > 0) & (step < STEPS - 1))
        def _():
            advect_tiles(range(TILES), *buffers)

        @pl.when(step == STEPS - 1)
        def _():
            advect_tiles(range(1, 1 + ROWS // 8), *buffers, wings=False)

        return 0

    lax.fori_loop(0, STEPS, one_step, 0)

    for tracer in range(TRACERS):
        flux = prior[tracer, :, mine].astype(jnp.float32)
        for step in range(STEPS):
            weights[step * TRACERS + tracer] = weights[step * TRACERS + tracer] * flux
        for level in range(HERE):
            kept[tracer, level] = field_ref[tracer, k * HERE + level, mid, main]
            returned[tracer, level] = field_ref[tracer, (1 - k) * HERE + level, mid, main]


def regions(side, weights, ids, sums, onehot, coarse, fine):
    mine = half_at(side[0])
    count = STEPS * TRACERS
    which = lax.broadcasted_iota(jnp.int32, (HI, HALF), 0)
    blank = jnp.zeros((SLOT - count, HALF), jnp.float32)
    nothing = jnp.zeros((SLOT, HALF), jnp.float32)
    for row in range(ROWS):
        at = slice(row * HALF, (row + 1) * HALF)
        region = ids[row : row + 1, mine]
        onehot[:, at] = jnp.where(which == region // LO, 1.0, 0.0).astype(jnp.bfloat16)
        value = jnp.concatenate([weights[:, row, :], blank], axis=0)
        big = value.astype(jnp.bfloat16).astype(jnp.float32)
        small = value - big
        for low in range(LO):
            here = region % LO == low
            to = slice(low * SLOT, (low + 1) * SLOT)
            coarse[to, at] = jnp.where(here, big, nothing).astype(jnp.bfloat16)
            fine[to, at] = jnp.where(here, small, nothing).astype(jnp.bfloat16)
    dims = (((1,), (1,)), ((), ()))
    total = lax.dot_general(onehot[...], coarse[...], dims, preferred_element_type=jnp.float32)
    total = total + lax.dot_general(onehot[...], fine[...], dims, preferred_element_type=jnp.float32)
    sums[pl.ds(0, HI, stride=2)] = total[:, :HALF]
    sums[pl.ds(1, HI, stride=2)] = total[:, HALF:]


def join(side, kept, received, out):
    k = side[0]
    for tracer in range(TRACERS):
        for level in range(HERE):
            out[tracer, level, :, half_at(k)] = kept[tracer, level]
            out[tracer, level, :, half_at(1 - k)] = received[tracer, level]


def body(adjoint, courant_lon, courant_lat, mixing, injection, prior_flux, region_ids):
    lon_count = lax.axis_size("lon")
    lat_count = lax.axis_size("lat")
    side = lax.axis_index("lev").astype(jnp.int32).reshape(1)
    raw = tuple(
        pltpu.with_memory_space_constraint(x, pltpu.HBM) for x in (adjoint, courant_lon, courant_lat, mixing)
    )
    own = tuple(hold(x) for x in (adjoint, courant_lon, courant_lat, mixing))
    far_injection = pltpu.with_memory_space_constraint(injection, pltpu.HBM)
    injection = hold(injection)

    strip = MAIN + FIELDS
    _, edge_cross, edge_same, edge_near, to_partner, first, last = call(
        pack,
        (
            *(near(FIELDS, FOLD, HALF) for _ in range(4)),
            near(PLANES, ROWS, HALF),
            near(strip, EDGE, HALF),
            near(strip, EDGE, HALF),
        ),
        (side, far_injection, *raw),
        1,
    )
    same = []
    cross = []
    for i in range(lon_count):
        after = (i + 1) % lon_count
        same += [(2 * i, 2 * after), (2 * after + 1, 2 * i + 1)]
        cross += [(2 * i + 1, 2 * after), (2 * after, 2 * i + 1)]
    north = [(j, j + 1) for j in range(lat_count - 1)]
    south = [(j + 1, j) for j in range(lat_count - 1)]
    lon_cross = permute(edge_cross, ("lon", "lev"), cross)
    lon_same = permute(edge_same, ("lon", "lev"), same)

    partner = permute(to_partner, "lev", [(0, 1), (1, 0)])
    own_below = permute(last, "lat", north)
    own_above = permute(first, "lat", south)

    strip = MAIN + 3 * FIELDS
    first, last = call(
        strips,
        (near(strip, EDGE, HALF), near(strip, EDGE, HALF)),
        (partner, lon_same, lon_cross, own_below, own_above),
        0,
    )
    below = permute(last, "lat", north)
    above = permute(first, "lat", south)

    block = (LEVELS, TALL, WIDE)
    tile = pltpu.VMEM((TRACERS, LEVELS, 8, WIDE), jnp.float32)
    arrays = (near(TRACERS, *block), near(TRACERS, *block), *(near(*block) for _ in range(5)))
    *state, inj = call(
        prepare,
        (*arrays, near(TRACERS, LEVELS, 8, HALF)),
        (side, injection, *own, partner, edge_near, lon_same, lon_cross),
        1,
        [tile],
    )
    kept, returned, weights = call(
        steps,
        (
            near(TRACERS, HERE, ROWS, HALF),
            near(TRACERS, HERE, ROWS, HALF),
            near(STEPS * TRACERS, ROWS, HALF),
            *arrays,
        ),
        (side, own_below, own_above, below, above, hold(prior_flux), hold(inj), *(hold(x) for x in state)),
        1,
        [tile],
        8,
        {7 + i: 3 + i for i in range(7)},
    )[:3]
    received = permute(returned, "lev", [(0, 1), (1, 0)])
    sums = call(
        regions,
        near(2 * HI, HALF),
        (side, weights, region_ids),
        1,
        [pltpu.VMEM((HI, ROWS * HALF), jnp.bfloat16) for _ in range(3)],
        12,
    )
    pieces = lax.all_to_all(sums, ("lon", "lat", "lev"), 0, 0, tiled=True)
    region_grad = jnp.sum(pieces, axis=0).reshape(-1, SLOT)[:, : STEPS * TRACERS]
    adjoint_out = call(join, f32(*adjoint.shape), (side, kept, received), 1)
    return (adjoint_out, region_grad)


def solution(mesh):
    placed = (
        P(None, "lev", "lat", "lon"),
        P("lev", "lat", "lon"),
        P("lev", "lat", "lon"),
        P("lev", "lat", "lon"),
        P(None, "lev"),
        P(None, "lat", "lon"),
        P("lat", "lon"),
    )
    return jax.shard_map(
        body,
        mesh=mesh,
        in_specs=placed,
        out_specs=(P(None, "lev", "lat", "lon"), P(("lon", "lat", "lev"), None)),
        check_vma=False,
    )
```
